32 devices in a mesh: seq: 16 (over z, y, x), head: 2 (over core).
Axes of the slice: x: 2, y: 2, z: 4, core: 2. Of those that a mesh axis runs over, the one named last changes fastest.
Arguments:
- queries: bfloat16 [4096, 5120], P('seq', 'head'), may hold values from -100 to 100
- keys: bfloat16 [4096, 5120], P('seq', 'head'), may hold values from -12 to 12
- values: bfloat16 [4096, 5120], P('seq', 'head'), may hold values from -6 to 6
- hidden: bfloat16 [4096, 5120], P('seq', 'head'), may hold values from -3 to 3
- cached: bfloat16 [4096, 5120], P('seq', 'head'), may hold values from -6 to 6
- active: int32 [4096], P('seq'), may hold values from 0 to 1, as said below
- w_out: bfloat16 [5120, 5120], P('head', 'seq'), may hold values from -0.078125 to 0.078125
Outputs:
- block_output: bfloat16 [4096, 5120], P('seq', 'head')
The draws below stay inside these ranges and needn't reach their ends.
Inputs may be any that keep to these rules, and one draw needn't show every extreme that they name: `active`: exactly 176 ones in all; among the 256 tokens of one index of seq at most 32 ones, and that many on some of them.
All inputs are finite; a program needn't handle non-finite values.
Results may differ from the reference program's by a relative error of at most 0.0039.
Values may be sent and summed in bfloat16 or wider, within the bound.
No kernel may reach another device: no remote copies, remote signals or barrier semaphores. Data moves between devices by JAX's collectives and lax.ppermute only.
A program may use at most 64 MiB of HBM per device.

```python
import jax
import jax.numpy as jnp
from jax import lax

D = 5120
HEADS = 40
HD = 128
TOK_DEV = 256
TOTAL_ACT = 176
TOKENS = 4096


def shared_base(key):
    return 1.6 * jax.random.normal(jax.random.fold_in(key, 11), (TOKENS, D), jnp.float32)


def draw_keys(key, part):
    result = shared_base(key)
    return jnp.clip(result, -12.0, 12.0).astype(jnp.bfloat16)


def draw_queries(key, part):
    result = 1.6 * jax.random.normal(jax.random.fold_in(key, 13), (TOKENS, D), jnp.float32)
    return jnp.clip(result, -100.0, 100.0).astype(jnp.bfloat16)


def draw_active(key, part):
    blocks = TOKENS // TOK_DEV
    capacity = TOK_DEV // 8
    device_order = jax.random.permutation(jax.random.fold_in(key, 3), blocks)
    counts = jnp.where(device_order < blocks // 8, capacity, capacity // 4)
    subkeys = jax.random.split(jax.random.fold_in(key, 5), blocks)
    ranking = jax.vmap(lambda subkey: jax.random.permutation(subkey, TOK_DEV))(subkeys)
    return (ranking < counts[:, None]).astype(jnp.int32).reshape(TOKENS)


def level_of(rng, shape, shards, least, top_value):
    def one(axis_at, blocks):
        heights = jax.random.uniform(jax.random.fold_in(jax.random.fold_in(rng, 6), axis_at), (blocks,), jnp.float32, least / len(shards), top_value / len(shards))
        return jnp.repeat(jnp.exp(heights), shape[axis_at] // blocks).reshape((-1,) + (1,) * (len(shape) - axis_at - 1))

    factor_of = one(*shards[0])
    for cut in shards[1:]:
        factor_of = factor_of * one(*cut)
    return factor_of


def scatter_about(own_key, shape, deviation, limit, shards=(), kind=jnp.bfloat16):
    values = jax.random.normal(own_key, shape, jnp.float32) * deviation
    if len(shards) > 0:
        values = level_of(own_key, shape, shards, -0.22, 0.18) * values
    return jnp.clip(values, min=-limit, max=limit).astype(kind)


def setup_inputs(seed: int = 0) -> dict:
    key_list = jax.random.split(jax.random.key(seed), 8)
    queries = draw_queries(jax.random.fold_in(key_list[7], 71), 0)
    keys = draw_keys(jax.random.fold_in(key_list[7], 71), 0)
    values = scatter_about(key_list[2], (TOKENS, D), 1.0, 6.0, ((0, 16), (1, 2)))
    hidden = scatter_about(key_list[3], (TOKENS, D), 0.5, 3.0, ((0, 16), (1, 2)))
    cached = scatter_about(key_list[4], (TOKENS, D), 1.0, 6.0, ((0, 16), (1, 2)))
    active = draw_active(jax.random.fold_in(key_list[7], 71), 0)
    w_out = scatter_about(key_list[6], (D, D), D ** -0.5, 0.078125, ((0, 2), (1, 16)))
    return dict(queries=queries, keys=keys, values=values, hidden=hidden, cached=cached, active=active, w_out=w_out)


def reference(queries, keys, values, hidden, cached, active, w_out):
    act_rows = jnp.nonzero(active, size=TOTAL_ACT, fill_value=0)[0].astype(jnp.int32)
    picked = queries[act_rows]
    blocks = TOKENS // TOK_DEV
    inv_root = 1.0 / (HD ** 0.5)

    def one_head(head):
        start = head * HD
        q_head = lax.dynamic_slice_in_dim(picked, start, HD, 1)
        k_head = lax.dynamic_slice_in_dim(keys, start, HD, 1)
        v_head = lax.dynamic_slice_in_dim(values, start, HD, 1)
        scores = jnp.dot(q_head, k_head.T, preferred_element_type=jnp.float32) * inv_root
        scores = scores.reshape(TOTAL_ACT, blocks, TOK_DEV)
        peak = jnp.max(scores, axis=2)
        expo = jnp.exp(scores - peak[:, :, None])
        total = jnp.sum(expo, axis=2)
        probs = expo.astype(jnp.bfloat16)
        partial_out = jnp.einsum("anb,nbd->and", probs.astype(jnp.float32),
                                 v_head.reshape(blocks, TOK_DEV, HD).astype(jnp.float32))
        partial_out = (partial_out / total[:, :, None]).astype(jnp.bfloat16)
        top_max = jnp.max(peak, axis=1, keepdims=True)
        weight = total * jnp.exp(peak - top_max)
        mixed = jnp.einsum("an,and->ad", weight, partial_out.astype(jnp.float32))
        return mixed / jnp.sum(weight, axis=1)[:, None]

    per_head = lax.map(one_head, jnp.arange(HEADS, dtype=jnp.int32))
    attn = jnp.transpose(per_head, (1, 0, 2)).reshape(TOTAL_ACT, D).astype(jnp.bfloat16)
    proj = jnp.dot(attn, w_out, preferred_element_type=jnp.float32)
    updated = (hidden[act_rows].astype(jnp.float32) + proj).astype(jnp.bfloat16)
    return cached.at[act_rows].set(updated)
```

```python
import functools
import math

import jax
import jax.numpy as jnp
from jax import lax
from jax.experimental import pallas as pl
from jax.experimental.pallas import tpu as pltpu
from jax.sharding import PartitionSpec as P

HD = 128
TILE = 16
LOG_LANES = 32
F32 = jnp.float32
BF16 = jnp.bfloat16
VMEM = pl.BlockSpec(memory_space=pltpu.VMEM)
LANES_BOTH = (((1,), (1,)), ((), ()))
ROWS_BOTH = (((0,), (0,)), ((), ()))


def iota(shape, dim):
    return lax.broadcasted_iota(jnp.int32, shape, dim).astype(F32)


class Plan:
    def __init__(self, devices, tok_dev, features):
        self.devices = devices
        self.heads = features // HD
        self.cap = tok_dev // 8
        self.total = devices * tok_dev * 11 // 256
        groups = -(-self.total // TILE)
        self.tok = groups * TILE
        self.whole = self.heads // devices
        self.rest = self.heads - self.whole * devices
        self.per_rest = devices // self.rest if self.rest else 0
        self.part = -(-groups // self.per_rest) * TILE if self.rest else 0
        self.rows = self.whole * self.tok + self.part
        self.slices = self.whole + (1 if self.rest else 0)
        self.sent = self.slices * self.cap + 8
        assert self.rows // TILE <= LOG_LANES

    def rest_of(self, device):
        return min(device // self.per_rest, self.rest - 1)

    def head_rows(self, ref, head):
        if head < self.whole * self.devices:
            first = head // self.devices * self.tok
            return ref[head % self.devices, first : first + self.tok, :]
        first = (head - self.whole * self.devices) * self.per_rest
        parts = [ref[first + i, self.whole * self.tok : self.rows, :] for i in range(self.per_rest)]
        return jnp.concatenate(parts, axis=0)[: self.tok]


def own_selection(act_ref, cap):
    tokens = act_ref.shape[1]
    act = act_ref[...].astype(F32)
    before = (iota((tokens, tokens), 0) < iota((tokens, tokens), 1)).astype(BF16)
    many = jnp.broadcast_to(act, (TILE, tokens)).astype(BF16)
    rank = jnp.dot(many, before, preferred_element_type=F32)[0:1]
    rank = jnp.where(act > 0, rank, -1.0)
    return (iota((cap, tokens), 0) == rank).astype(BF16), act


def select_kernel(plan, act_ref, q_ref, out_ref):
    chosen, act = own_selection(act_ref, plan.cap)
    count = jnp.broadcast_to(jnp.sum(act, axis=1, keepdims=True), (8, HD)).astype(BF16)
    own = jnp.dot(chosen, q_ref[...], preferred_element_type=F32).astype(BF16)
    for device in range(plan.devices):
        heads = [i * plan.devices + device for i in range(plan.whole)]
        if plan.rest:
            heads.append(plan.whole * plan.devices + plan.rest_of(device))
        for i, head in enumerate(heads):
            out_ref[device, i * plan.cap : (i + 1) * plan.cap, :] = own[:, head * HD : (head + 1) * HD]
        out_ref[device, plan.slices * plan.cap :, :] = count


def compact_kernel(plan, where_ref, in_ref, out_ref, info_ref):
    devices, cap = plan.devices, plan.cap
    count = jnp.max(in_ref[:, plan.slices * cap :, :].astype(F32), axis=1)
    earlier = (iota((devices, devices), 1) < iota((devices, devices), 0)).astype(BF16)
    offset = jnp.dot(earlier, count.astype(BF16), preferred_element_type=F32)
    info_ref[0] = count
    info_ref[1] = offset
    slots = devices * cap
    place = iota((devices, slots), 1) - iota((devices, slots), 0) * cap
    held = (place >= 0) & (place < jnp.minimum(count[:, 0:1], float(cap)))
    rank = jnp.sum(jnp.where(held, offset[:, 0:1] + place + 1.0, 0.0), axis=0, keepdims=True) - 1.0

    def put(first, rows, base, index):
        pick = (iota((rows, slots), 0) + base == rank).astype(BF16)
        source = in_ref[:, index * cap : (index + 1) * cap, :].reshape(slots, HD)
        packed = jnp.dot(pick, source, preferred_element_type=F32).astype(BF16)
        for device in range(devices):
            out_ref[device, first : first + rows, :] = packed

    for i in range(plan.whole):
        put(i * plan.tok, plan.tok, 0.0, i)
    if plan.rest:
        me = where_ref[0]
        index = me - jnp.minimum(me // plan.per_rest, plan.rest - 1) * plan.per_rest
        put(plan.whole * plan.tok, plan.part, (index * plan.part).astype(F32), plan.whole)


def spread_logs(logs, first, count):
    lane = lax.broadcasted_iota(jnp.int32, (TILE, HD), 1)
    laid = jnp.zeros((TILE, HD), F32)
    for i in range(count):
        laid = jnp.where(lane == first + i, logs[i * TILE : (i + 1) * TILE], laid)
    high = laid.astype(BF16).astype(F32)
    mid = (laid - high).astype(BF16).astype(F32)
    low = (laid - high - mid).astype(BF16).astype(F32)
    return (high + pltpu.roll(mid, LOG_LANES, 1) + pltpu.roll(low, 2 * LOG_LANES, 1)).astype(BF16)


def attention_kernel(plan, q_ref, k_ref, v_ref, out_ref):
    devices, tok, part = plan.devices, plan.tok, plan.part
    inv_root = 1.0 / HD**0.5
    tail = plan.whole * tok

    def attend(query, head):
        columns = pl.ds(pl.multiple_of(head * HD, HD), HD)
        scores = (
            lax.dot_general(query, k_ref[:, columns], LANES_BOTH, preferred_element_type=F32)
            * inv_root
        )
        peak = jnp.max(scores, axis=1, keepdims=True)
        expo = jnp.exp(scores - peak)
        total = jnp.sum(expo, axis=1, keepdims=True)
        block = jnp.dot(expo.astype(BF16), v_ref[:, columns], preferred_element_type=F32)
        return (block / total).astype(BF16), peak + jnp.log(total)

    if plan.rest * plan.per_rest < devices or not plan.whole:
        out_ref[...] = jnp.zeros_like(out_ref)
    for i in range(plan.whole):
        def whole_head(device, carry, i=i):
            result, logs = attend(q_ref[device, i * tok : (i + 1) * tok, :], device + i * devices)
            out_ref[device, i * tok : (i + 1) * tok, :] = result
            laid = spread_logs(logs, i * (tok // TILE), tok // TILE)
            if i:
                laid = out_ref[device, plan.rows :, :] + laid
            out_ref[device, plan.rows :, :] = laid
            return carry

        lax.fori_loop(0, devices, whole_head, 0, unroll=2)

    def rest_head(index, carry):
        first = index * plan.per_rest
        query = jnp.concatenate(
            [q_ref[first + j, tail : plan.rows, :] for j in range(plan.per_rest)], axis=0
        )
        result, logs = attend(query, index + plan.whole * devices)
        for j in range(plan.per_rest):
            mine = slice(j * part, (j + 1) * part)
            out_ref[first + j, tail : plan.rows, :] = result[mine]
            laid = spread_logs(logs[mine], tail // TILE, part // TILE)
            out_ref[first + j, plan.rows :, :] = out_ref[first + j, plan.rows :, :] + laid
        return carry

    if plan.rest:
        lax.fori_loop(0, plan.rest, rest_head, 0)


def combine_kernel(plan, in_ref, out_ref, weight_ref):
    devices, rows = plan.devices, plan.rows

    def logs(device):
        kept = in_ref[device, rows:, :].astype(F32)
        return (
            kept
            + pltpu.roll(kept, HD - LOG_LANES, 1)
            + pltpu.roll(kept, HD - 2 * LOG_LANES, 1)
        )

    top = logs(0)
    for device in range(1, devices):
        top = jnp.maximum(top, logs(device))
    total = jnp.zeros((TILE, HD), F32)
    for device in range(devices):
        weight = jnp.exp(logs(device) - top)
        weight_ref[device] = weight
        total = total + weight
    scale = 1.0 / total

    def add(device, carry):
        weight = weight_ref[device] * scale
        return tuple(
            held
            + weight[:, i : i + 1] * in_ref[device, i * TILE : (i + 1) * TILE, :].astype(F32)
            for i, held in enumerate(carry)
        )

    start = tuple(jnp.zeros((TILE, HD), F32) for _ in range(rows // TILE))
    done = lax.fori_loop(0, devices, add, start, unroll=2)
    for i, held in enumerate(done):
        block = held.astype(BF16)
        for device in range(devices):
            out_ref[device, i * TILE : (i + 1) * TILE, :] = block


def project_kernel(plan, attn_ref, w_ref, info_ref, out_ref):
    devices, cap, tok = plan.devices, plan.cap, plan.tok
    attn = jnp.concatenate([plan.head_rows(attn_ref, h) for h in range(plan.heads)], axis=1)
    proj = lax.dot_general(attn, w_ref[...], LANES_BOTH, preferred_element_type=F32).astype(BF16)
    picks = []
    for device in range(devices):
        place = iota((cap, tok), 0)
        count = info_ref[0, device : device + 1, 0:1]
        offset = info_ref[1, device : device + 1, 0:1]
        picks.append(
            ((iota((cap, tok), 1) - offset == place) & (place < count)).astype(F32).astype(BF16)
        )
    pick = jnp.concatenate(picks, axis=0)
    laid = jnp.dot(pick, proj, preferred_element_type=F32).astype(BF16)
    out_ref[...] = laid.reshape(devices, cap, w_ref.shape[0])


def update_kernel(cap, act_ref, *refs):
    *term_refs, hidden_ref, cached_ref, out_ref = refs
    chosen, _ = own_selection(act_ref, cap)
    mask = lax.dot_general(chosen, jnp.ones((cap, HD), BF16), ROWS_BOTH, preferred_element_type=F32)
    terms = []
    for ref in term_refs:
        for i in range(ref.shape[0]):
            wide = [ref[i, j].astype(F32) for j in range(ref.shape[1])]
            terms.append(jnp.concatenate(wide, axis=1).astype(BF16))
    many = jnp.concatenate([chosen] * len(terms), axis=0)
    summed = lax.dot_general(
        many, jnp.concatenate(terms, axis=0), ROWS_BOTH, preferred_element_type=F32
    )
    updated = (hidden_ref[...].astype(F32) + summed).astype(BF16)
    out_ref[...] = jnp.where(mask[:, 0:1] > 0, updated, cached_ref[...])


def call(kernel, name, out_shape, *args, **options):
    return pl.pallas_call(
        kernel,
        name=name,
        out_shape=out_shape,
        in_specs=options.pop("in_specs", [VMEM] * len(args)),
        out_specs=options.pop("out_specs", jax.tree.map(lambda _: VMEM, out_shape)),
        compiler_params=pltpu.CompilerParams(vmem_limit_bytes=48 << 20),
        **options,
    )(*args)


def exchange(value):
    return lax.all_to_all(value, "seq", split_axis=0, concat_axis=0, tiled=True)


def shards(queries, keys, values, hidden, cached, active, w_out):
    tok_dev, features = queries.shape
    devices, halves = lax.axis_size("seq"), lax.axis_size("head")
    plan = Plan(devices, tok_dev, features)
    cap = plan.cap
    act = active.reshape(1, tok_dev)
    shape = jax.ShapeDtypeStruct
    me = lax.axis_index("seq").astype(jnp.int32).reshape(1)

    sent = call(
        functools.partial(select_kernel, plan), "select",
        shape((devices, plan.sent, HD), BF16), act, queries,
    )
    chunk, info = call(
        functools.partial(compact_kernel, plan), "compact",
        (shape((devices, plan.rows, HD), BF16), shape((2, devices, HD), F32)),
        me, exchange(sent),
        in_specs=[pl.BlockSpec(memory_space=pltpu.SMEM), VMEM],
    )
    partials = call(
        functools.partial(attention_kernel, plan), "attend",
        shape((devices, plan.rows + TILE, HD), BF16), exchange(chunk), keys, values,
    )
    mixed = call(
        functools.partial(combine_kernel, plan), "combine",
        shape((devices, plan.rows, HD), BF16), exchange(partials),
        scratch_shapes=[pltpu.VMEM((devices, TILE, HD), F32)],
    )
    columns = w_out.shape[1]
    terms = call(
        functools.partial(project_kernel, plan), "project",
        shape((devices, cap, columns), BF16), exchange(mixed), w_out.T, info,
    )
    arrived = exchange(terms)

    half = lax.axis_index("head").astype(jnp.int32).reshape(1)
    wide = math.lcm(columns, HD)
    blocks = wide // columns
    steps = features // wide
    if halves == 2:
        other = lax.ppermute(arrived, "head", [(0, 1), (1, 0)])
        term_args = [arrived[None], other[None]]
        term_spec = pl.BlockSpec((1, blocks, cap, columns), lambda i, h: (0, h[0] * steps + i, 0, 0))
    else:
        split = arrived.reshape(halves, devices // halves, cap, columns)
        term_args = [lax.all_to_all(split, "head", split_axis=0, concat_axis=0, tiled=True)]
        term_spec = pl.BlockSpec((halves, blocks, cap, columns), lambda i, h: (0, i, 0, 0))
    column_spec = pl.BlockSpec((tok_dev, wide), lambda i, h: (0, i))

    def update(half_ref, *refs):
        update_kernel(cap, *refs)

    return pl.pallas_call(
        update,
        name="update",
        out_shape=shape((tok_dev, features), BF16),
        grid_spec=pltpu.PrefetchScalarGridSpec(
            num_scalar_prefetch=1,
            grid=(steps,),
            in_specs=[
                pl.BlockSpec((1, tok_dev), lambda i, h: (0, 0)),
                *[term_spec] * len(term_args),
                column_spec,
                column_spec,
            ],
            out_specs=column_spec,
        ),
    )(half, act, *term_args, hidden, cached)


def solution(mesh):
    placed = (
        P("seq", "head"),
        P("seq", "head"),
        P("seq", "head"),
        P("seq", "head"),
        P("seq", "head"),
        P("seq"),
        P("head", "seq"),
    )
    return jax.shard_map(
        shards, mesh=mesh, in_specs=placed, out_specs=P("seq", "head"), check_vma=False
    )
```

```python
import functools
import math

import jax
import jax.numpy as jnp
from jax import lax
from jax.experimental import pallas as pl
from jax.experimental.pallas import tpu as pltpu
from jax.sharding import PartitionSpec as P

HD = 128
TILE = 16
QUAD = 4
LOG_LANES = 32
F32 = jnp.float32
BF16 = jnp.bfloat16
VMEM = pl.BlockSpec(memory_space=pltpu.VMEM)
SMEM = pl.BlockSpec(memory_space=pltpu.SMEM)
LANES_BOTH = (((1,), (1,)), ((), ()))
ROWS_BOTH = (((0,), (0,)), ((), ()))


def iota(shape, dim):
    return lax.broadcasted_iota(jnp.int32, shape, dim).astype(F32)


class Plan:
    def __init__(self, devices, tok_dev, features):
        assert devices % (2 * QUAD) == 0
        self.devices = devices
        self.line = devices // QUAD
        self.heads = features // HD
        self.own_heads = -(-self.heads // QUAD)
        self.cap = tok_dev // 8
        self.total = devices * tok_dev * 11 // 256
        groups = -(-self.total // TILE)
        self.tok = groups * TILE
        self.tiles = -(-self.own_heads * groups // self.line)
        self.rows = self.tiles * TILE
        self.half = self.line // 2 * self.rows
        assert self.tiles <= LOG_LANES

    def head_at(self, index, quad):
        return jnp.minimum(index * QUAD + quad, self.heads - 1)

    def head_rows(self, refs, index):
        first, last = index * self.tok, (index + 1) * self.tok
        parts = []
        for i, ref in enumerate(refs):
            low, high = max(first - i * self.half, 0), min(last - i * self.half, self.half)
            if low < high:
                parts.append(ref[low:high, :])
        return parts[0] if len(parts) == 1 else jnp.concatenate(parts, axis=0)

    def put_rows(self, refs, index, block):
        first, last = index * self.tok, (index + 1) * self.tok
        for i, ref in enumerate(refs):
            low, high = max(first, i * self.half), min(last, (i + 1) * self.half)
            if low < high:
                ref[low - i * self.half : high - i * self.half, :] = block[low - first : high - first]


def own_selection(act_ref, cap):
    tokens = act_ref.shape[1]
    act = act_ref[...].astype(F32)
    before = (iota((tokens, tokens), 0) < iota((tokens, tokens), 1)).astype(BF16)
    many = jnp.broadcast_to(act, (TILE, tokens)).astype(BF16)
    rank = jnp.dot(many, before, preferred_element_type=F32)[0:1]
    rank = jnp.where(act > 0, rank, -1.0)
    return (iota((cap, tokens), 0) == rank).astype(BF16), act


def select_kernel(plan, act_ref, q_ref, out_ref):
    chosen, act = own_selection(act_ref, plan.cap)
    count = jnp.broadcast_to(jnp.sum(act, axis=1, keepdims=True), (8, HD)).astype(BF16)
    own = jnp.dot(chosen, q_ref[...], preferred_element_type=F32).astype(BF16)
    for device in range(plan.devices):
        for i in range(plan.own_heads):
            head = min(i * QUAD + device % QUAD, plan.heads - 1)
            out_ref[device, i * plan.cap : (i + 1) * plan.cap, :] = own[:, head * HD : (head + 1) * HD]
        out_ref[device, plan.own_heads * plan.cap :, :] = count


def compact_kernel(plan, in_ref, low_ref, high_ref, info_ref):
    devices, cap = plan.devices, plan.cap
    count = jnp.max(in_ref[:, plan.own_heads * cap :, :].astype(F32), axis=1)
    earlier = (iota((devices, devices), 1) < iota((devices, devices), 0)).astype(BF16)
    offset = jnp.dot(earlier, count.astype(BF16), preferred_element_type=F32)
    info_ref[0] = count
    info_ref[1] = offset
    slots = devices * cap
    place = iota((devices, slots), 1) - iota((devices, slots), 0) * cap
    held = (place >= 0) & (place < jnp.minimum(count[:, 0:1], float(cap)))
    rank = jnp.sum(jnp.where(held, offset[:, 0:1] + place + 1.0, 0.0), axis=0, keepdims=True) - 1.0
    pick = (iota((plan.tok, slots), 0) == rank).astype(BF16)
    rest = plan.line * plan.rows - plan.own_heads * plan.tok
    if rest:
        high_ref[plan.half - rest :, :] = jnp.zeros((rest, HD), BF16)
    for i in range(plan.own_heads):
        source = in_ref[:, i * cap : (i + 1) * cap, :].reshape(slots, HD)
        packed = jnp.dot(pick, source, preferred_element_type=F32).astype(BF16)
        plan.put_rows((low_ref, high_ref), i, packed)


def pack_logs(logs):
    high = logs.astype(BF16).astype(F32)
    mid = (logs - high).astype(BF16).astype(F32)
    low = (logs - high - mid).astype(BF16).astype(F32)
    return (high + pltpu.roll(mid, LOG_LANES, 1) + pltpu.roll(low, 2 * LOG_LANES, 1)).astype(BF16)


def unpack_logs(packed):
    kept = packed.astype(F32)
    return kept + pltpu.roll(kept, HD - LOG_LANES, 1) + pltpu.roll(kept, HD - 2 * LOG_LANES, 1)


def attention_kernel(plan, step, where_ref, low_ref, high_ref, k_ref, v_ref, out_ref):
    inv_root = 1.0 / HD**0.5
    quad = (where_ref[0] & (QUAD - 1)) ^ step
    lane = lax.broadcasted_iota(jnp.int32, (TILE, HD), 1)
    laid = [jnp.zeros((TILE, HD), F32) for _ in range(plan.line)]
    rest = plan.line * plan.rows - plan.own_heads * plan.tok
    if rest:
        first = plan.own_heads * plan.tok
        for chunk in range(first // plan.rows, plan.line):
            low = max(first - chunk * plan.rows, 0)
            out_ref[chunk, low : plan.rows, :] = jnp.zeros((plan.rows - low, HD), BF16)
    for i in range(plan.own_heads):
        columns = pl.ds(pl.multiple_of(plan.head_at(i, quad) * HD, HD), HD)
        query = plan.head_rows((low_ref, high_ref), i)
        scores = (
            lax.dot_general(query, k_ref[:, columns], LANES_BOTH, preferred_element_type=F32)
            * inv_root
        )
        peak = jnp.max(scores, axis=1, keepdims=True)
        expo = jnp.exp(scores - peak)
        total = jnp.sum(expo, axis=1, keepdims=True)
        block = jnp.dot(expo.astype(BF16), v_ref[:, columns], preferred_element_type=F32)
        block = (block / total).astype(BF16)
        logs = peak + jnp.log(total)
        for tile in range(plan.tok // TILE):
            chunk, place = divmod(i * (plan.tok // TILE) + tile, plan.tiles)
            mine = slice(tile * TILE, (tile + 1) * TILE)
            out_ref[chunk, place * TILE : (place + 1) * TILE, :] = block[mine]
            laid[chunk] = jnp.where(lane == place, logs[mine], laid[chunk])
    for chunk in range(plan.line):
        out_ref[chunk, plan.rows :, :] = pack_logs(laid[chunk])


def merge(plan, parts, out_ref, keep_logs):
    rows = plan.rows
    logs = [unpack_logs(part[rows:, :]) for part in parts]
    top = functools.reduce(jnp.maximum, logs)
    weights = [jnp.exp(log - top) for log in logs]
    total = functools.reduce(jnp.add, weights)
    scale = 1.0 / total
    weights = [weight * scale for weight in weights]
    for tile in range(plan.tiles):
        mine = slice(tile * TILE, (tile + 1) * TILE)
        mixed = functools.reduce(
            jnp.add,
            [w[:, tile : tile + 1] * part[mine, :].astype(F32) for w, part in zip(weights, parts)],
        )
        out_ref[mine, :] = mixed.astype(BF16)
    if keep_logs:
        lane = lax.broadcasted_iota(jnp.int32, (TILE, HD), 1)
        out_ref[rows:, :] = pack_logs(jnp.where(lane < LOG_LANES, top + jnp.log(total), 0.0))


def quad_kernel(plan, where_ref, *refs):
    parts, outs = refs[:QUAD], refs[QUAD:]
    line = where_ref[0] // QUAD
    for step, out_ref in enumerate(outs):
        merge(plan, [part.at[line ^ step] for part in parts], out_ref, True)


def line_kernel(plan, *refs):
    merge(plan, refs[:-1], refs[-1], False)


def stack_kernel(plan, where_ref, *refs):
    *parts, low_ref, high_ref, held_ref = refs
    line = where_ref[0] // QUAD
    for step, part in enumerate(parts):
        held_ref[line ^ step] = part[...]
    for i in range(plan.line // 2):
        low_ref[i * plan.rows : (i + 1) * plan.rows, :] = held_ref[i]
        high_ref[i * plan.rows : (i + 1) * plan.rows, :] = held_ref[plan.line // 2 + i]


def project_group(plan, quad, refs, w_ref):
    sides, weights = [], []
    for i in range(plan.own_heads):
        block = plan.head_rows(refs, i)
        if plan.own_heads * QUAD != plan.heads:
            block = jnp.where(i * QUAD + quad < plan.heads, block, jnp.zeros_like(block))
        sides.append(block)
        columns = pl.ds(pl.multiple_of(plan.head_at(i, quad) * HD, HD), HD)
        weights.append(w_ref[:, columns])
    return lax.dot_general(
        jnp.concatenate(sides, axis=1),
        jnp.concatenate(weights, axis=1),
        LANES_BOTH,
        preferred_element_type=F32,
    )


def project_kernel(plan, steps, where_ref, w_ref, *refs):
    *refs, out_ref = refs
    total = None
    if len(refs) % 2:
        *refs, sum_ref = refs
        total = sum_ref[...]
    for i, step in enumerate(steps):
        quad = (where_ref[0] & (QUAD - 1)) ^ step
        term = project_group(plan, quad, refs[2 * i : 2 * i + 2], w_ref)
        total = term if total is None else total + term
    out_ref[...] = total


def place_kernel(plan, step, where_ref, w_ref, low_ref, high_ref, sum_ref, info_ref, out_ref):
    devices, cap, tok = plan.devices, plan.cap, plan.tok
    quad = (where_ref[0] & (QUAD - 1)) ^ step
    proj = sum_ref[...] + project_group(plan, quad, (low_ref, high_ref), w_ref)
    picks = []
    for device in range(devices):
        place = iota((cap, tok), 0)
        count = info_ref[0, device : device + 1, 0:1]
        offset = info_ref[1, device : device + 1, 0:1]
        picks.append(
            ((iota((cap, tok), 1) - offset == place) & (place < count)).astype(F32).astype(BF16)
        )
    pick = jnp.concatenate(picks, axis=0)
    laid = jnp.dot(pick, proj.astype(BF16), preferred_element_type=F32).astype(BF16)
    out_ref[...] = laid.reshape(devices, cap, w_ref.shape[0])


def update_kernel(cap, act_ref, *refs):
    *term_refs, hidden_ref, cached_ref, out_ref = refs
    chosen, _ = own_selection(act_ref, cap)
    mask = lax.dot_general(chosen, jnp.ones((cap, HD), BF16), ROWS_BOTH, preferred_element_type=F32)
    terms = []
    for ref in term_refs:
        for i in range(ref.shape[0]):
            wide = [ref[i, j].astype(F32) for j in range(ref.shape[1])]
            terms.append(jnp.concatenate(wide, axis=1).astype(BF16))
    many = jnp.concatenate([chosen] * len(terms), axis=0)
    summed = lax.dot_general(
        many, jnp.concatenate(terms, axis=0), ROWS_BOTH, preferred_element_type=F32
    )
    updated = (hidden_ref[...].astype(F32) + summed).astype(BF16)
    out_ref[...] = jnp.where(mask[:, 0:1] > 0, updated, cached_ref[...])


def shape(*dims, dtype=BF16):
    return jax.ShapeDtypeStruct(dims, dtype)


def call(kernel, name, out_shape, *args, cost=None, **options):
    return pl.pallas_call(
        kernel,
        name=name,
        out_shape=out_shape,
        in_specs=[SMEM if a.dtype == jnp.int32 and a.ndim == 1 else VMEM for a in args],
        out_specs=jax.tree.map(lambda _: VMEM, out_shape),
        compiler_params=pltpu.CompilerParams(vmem_limit_bytes=32 << 20),
        cost_estimate=cost,
        **options,
    )(*args)


def exchange(value):
    return lax.all_to_all(value, "seq", split_axis=0, concat_axis=0, tiled=True)


def shift(value, mask):
    pairs = [(i, i ^ mask) for i in range(lax.axis_size("seq"))]
    return lax.ppermute(value, "seq", pairs)


def quad_gather(low, high):
    x_low, y_high = shift(low, 1), shift(high, 2)
    x_high, y_low = shift(high, 1), shift(low, 2)
    return [(low, high), (x_low, x_high), (y_low, y_high), (shift(x_low, 2), shift(y_high, 1))]


def shards(queries, keys, values, hidden, cached, active, w_out):
    tok_dev, features = queries.shape
    devices, halves = lax.axis_size("seq"), lax.axis_size("head")
    plan = Plan(devices, tok_dev, features)
    cap, columns = plan.cap, w_out.shape[1]
    act = active.reshape(1, tok_dev)
    me = lax.axis_index("seq").astype(jnp.int32).reshape(1)
    halves_shape = (shape(plan.half, HD), shape(plan.half, HD))

    sent = call(
        functools.partial(select_kernel, plan), "select",
        shape(devices, plan.own_heads * cap + 8, HD), act, queries,
    )
    low, high, info = call(
        functools.partial(compact_kernel, plan), "compact",
        (*halves_shape, shape(2, devices, HD, dtype=F32)), exchange(sent),
    )
    scored = plan.own_heads * plan.tok * tok_dev
    cost = pl.CostEstimate(
        flops=4 * scored * HD, transcendentals=scored, bytes_accessed=4 * tok_dev * HD * plan.own_heads
    )
    partials = []
    for step, (a, b) in enumerate(quad_gather(low, high)):
        part = call(
            functools.partial(attention_kernel, plan, step), f"attend_{step}",
            shape(plan.line, plan.rows + TILE, HD), me, a, b, keys, values, cost=cost,
        )
        partials.append(shift(part, step) if step else part)
    sums = call(
        functools.partial(quad_kernel, plan), "merge_quad",
        tuple(shape(plan.rows + TILE, HD) for _ in range(plan.line)), me, *partials,
    )
    arrived = [shift(part, step * QUAD) if step else part for step, part in enumerate(sums)]
    chunk = call(functools.partial(line_kernel, plan), "merge_line", shape(plan.rows, HD), *arrived)
    line = [shift(chunk, step * QUAD) if step else chunk for step in range(plan.line)]
    low, high = call(
        functools.partial(stack_kernel, plan), "stack", halves_shape, me, *line,
        scratch_shapes=[pltpu.VMEM((plan.line, plan.rows, HD), BF16)],
    )
    w_rows = w_out.T
    cost = pl.CostEstimate(
        flops=2 * plan.own_heads * plan.tok * HD * columns,
        transcendentals=0,
        bytes_accessed=2 * plan.own_heads * HD * columns,
    )
    groups = quad_gather(low, high)
    proj = None
    for step in range(QUAD - 1):
        extra = () if proj is None else (proj,)
        proj = call(
            functools.partial(project_kernel, plan, (step,)), f"project_{step}",
            shape(plan.tok, columns, dtype=F32), me, w_rows, *groups[step], *extra, cost=cost,
        )
    terms = call(
        functools.partial(place_kernel, plan, QUAD - 1), "place",
        shape(devices, cap, columns), me, w_rows, *groups[QUAD - 1], proj, info,
    )
    arrived = exchange(terms)

    half = lax.axis_index("head").astype(jnp.int32).reshape(1)
    wide = math.lcm(columns, HD)
    blocks = wide // columns
    steps = features // wide
    if halves == 2:
        other = lax.ppermute(arrived, "head", [(0, 1), (1, 0)])
        term_args = [arrived[None], other[None]]
        term_spec = pl.BlockSpec((1, blocks, cap, columns), lambda i, h: (0, h[0] * steps + i, 0, 0))
    else:
        split = arrived.reshape(halves, devices // halves, cap, columns)
        term_args = [lax.all_to_all(split, "head", split_axis=0, concat_axis=0, tiled=True)]
        term_spec = pl.BlockSpec((halves, blocks, cap, columns), lambda i, h: (0, i, 0, 0))
    column_spec = pl.BlockSpec((tok_dev, wide), lambda i, h: (0, i))

    def update(half_ref, *refs):
        update_kernel(cap, *refs)

    return pl.pallas_call(
        update,
        name="update",
        out_shape=shape(tok_dev, features),
        grid_spec=pltpu.PrefetchScalarGridSpec(
            num_scalar_prefetch=1,
            grid=(steps,),
            in_specs=[
                pl.BlockSpec((1, tok_dev), lambda i, h: (0, 0)),
                *[term_spec] * len(term_args),
                column_spec,
                column_spec,
            ],
            out_specs=column_spec,
        ),
    )(half, act, *term_args, hidden, cached)


def solution(mesh):
    placed = (
        P("seq", "head"),
        P("seq", "head"),
        P("seq", "head"),
        P("seq", "head"),
        P("seq", "head"),
        P("seq"),
        P("head", "seq"),
    )
    return jax.shard_map(
        shards, mesh=mesh, in_specs=placed, out_specs=P("seq", "head"), check_vma=False
    )
```

```python
import functools
import math

import jax
import jax.numpy as jnp
from jax import lax
from jax.experimental import pallas as pl
from jax.experimental.pallas import tpu as pltpu
from jax.sharding import PartitionSpec as P


HD = 128
TILE = 16
QUAD = 4
LOG_LANES = 32
F32 = jnp.float32
BF16 = jnp.bfloat16
VMEM = pl.BlockSpec(memory_space=pltpu.VMEM)
SMEM = pl.BlockSpec(memory_space=pltpu.SMEM)
HBM = pl.BlockSpec(memory_space=pltpu.HBM)
LANES_BOTH = (((1,), (1,)), ((), ()))
ROWS_BOTH = (((0,), (0,)), ((), ()))


def iota(shape, dim):
    return lax.broadcasted_iota(jnp.int32, shape, dim).astype(F32)


class Plan:
    def __init__(self, devices, tok_dev, features):
        assert devices % (2 * QUAD) == 0
        self.devices = devices
        self.line = devices // QUAD
        self.heads = features // HD
        self.own_heads = -(-self.heads // QUAD)
        self.cap = tok_dev // 8
        self.total = devices * tok_dev * 11 // 256
        groups = -(-self.total // TILE)
        self.tok = groups * TILE
        self.tiles = -(-self.own_heads * groups // self.line)
        self.rows = self.tiles * TILE
        self.half = self.line // 2 * self.rows
        self.spans = max(
            min((self.tiles * (line + 1) - 1) // groups, self.own_heads - 1) - self.tiles * line // groups + 1
            for line in range(self.line)
        )
        assert self.tiles <= LOG_LANES

    def head_at(self, index, quad):
        return jnp.minimum(index * QUAD + quad, self.heads - 1)

    def first_head(self, line):
        return line * self.tiles * TILE // self.tok

    def sent_heads(self, device):
        first = self.first_head(device // QUAD)
        local = [min(first + i, self.own_heads - 1) for i in range(self.spans)]
        return [min(i * QUAD + device % QUAD, self.heads - 1) for i in local]

    def head_rows(self, refs, index):
        first, last = index * self.tok, (index + 1) * self.tok
        parts = []
        for i, ref in enumerate(refs):
            low, high = max(first - i * self.half, 0), min(last - i * self.half, self.half)
            if low < high:
                parts.append(ref[low:high, :])
        return parts[0] if len(parts) == 1 else jnp.concatenate(parts, axis=0)


def own_selection(act, cap):
    tokens = act.shape[1]
    before = (iota((tokens, tokens), 0) < iota((tokens, tokens), 1)).astype(BF16)
    many = jnp.broadcast_to(act, (TILE, tokens)).astype(BF16)
    rank = jnp.dot(many, before, preferred_element_type=F32)[0:1]
    rank = jnp.where(act > 0, rank, -1.0)
    return (iota((cap, tokens), 0) == rank).astype(BF16)


def prepare_kernel(plan, parts, wanted, act_hbm, q_hbm, k_hbm, v_hbm, *refs):
    out_ref, *fetched = refs[: 1 + len(wanted)]
    act_ref, q_ref, own_ref, passing, q_sems, in_sems, out_sems = refs[1 + len(wanted) :]
    me = lax.axis_index("seq")
    heads = plan.own_heads
    arriving, leaving = [], []
    for j, (source, step) in enumerate(wanted):
        quad = lax.rem(me, QUAD) ^ step
        for i in range(heads):
            columns = pl.ds(pl.multiple_of(plan.head_at(i, quad) * HD, HD), HD)
            n = j * heads + i
            taken = (k_hbm, v_hbm)[source].at[:, columns]
            target = fetched[j].at[:, i * HD : (i + 1) * HD]
            arriving.append(pltpu.make_async_copy(taken, passing.at[n], in_sems.at[n]))
            leaving.append(pltpu.make_async_copy(passing.at[n], target, out_sems.at[n]))
    wide = q_hbm.shape[1] // parts
    columns = [slice(i * wide, (i + 1) * wide) for i in range(parts)]
    queries = [
        pltpu.make_async_copy(q_hbm.at[:, c], q_ref.at[:, c], q_sems.at[i])
        for i, c in enumerate(columns)
    ]
    first = pltpu.make_async_copy(act_hbm, act_ref, q_sems.at[parts])
    early = 2 * heads
    for copy in [first, *arriving[:early], *queries, *arriving[early:]]:
        copy.start()

    def forward(low, high):
        for one, two in zip(arriving[low:high], leaving[low:high]):
            one.wait()
            two.start()

    first.wait()
    act = act_ref[...].astype(F32)
    chosen = own_selection(act, plan.cap)
    count = jnp.broadcast_to(jnp.sum(act, axis=1, keepdims=True), (8, HD)).astype(BF16)
    forward(0, early)
    for copy, c in zip(queries, columns):
        copy.wait()
        own_ref[:, c] = jnp.dot(chosen, q_ref[:, c], preferred_element_type=F32).astype(BF16)
    forward(early, len(arriving))
    for device in range(plan.devices):
        for i, head in enumerate(plan.sent_heads(device)):
            out_ref[device, i * plan.cap : (i + 1) * plan.cap, :] = own_ref[:, head * HD : (head + 1) * HD]
        out_ref[device, plan.spans * plan.cap :, :] = count
    for copy in leaving:
        copy.wait()


def compact_kernel(plan, where_ref, in_ref, out_ref, info_ref):
    devices, cap = plan.devices, plan.cap
    count = jnp.max(in_ref[:, plan.spans * cap :, :].astype(F32), axis=1)
    earlier = (iota((devices, devices), 1) < iota((devices, devices), 0)).astype(BF16)
    offset = jnp.dot(earlier, count.astype(BF16), preferred_element_type=F32)
    info_ref[0] = count
    info_ref[1] = offset
    slots = devices * cap
    place = iota((devices, slots), 1) - iota((devices, slots), 0) * cap
    held = (place >= 0) & (place < jnp.minimum(count[:, 0:1], float(cap)))
    ranks = jnp.sum(jnp.where(held, offset[:, 0:1] + place + 1.0, 0.0), axis=0, keepdims=True) - 1.0
    ranks = jnp.where(ranks < 0, -1.0e6, ranks)
    line = where_ref[0] // QUAD
    start = line * plan.rows - plan.first_head(line) * plan.tok
    packed = jnp.zeros((plan.rows, HD), F32)
    for i in range(plan.spans):
        token = iota((plan.rows, slots), 0) + (start - i * plan.tok).astype(F32)
        pick = (token == ranks).astype(BF16)
        source = in_ref[:, i * cap : (i + 1) * cap, :].reshape(slots, HD)
        packed = packed + jnp.dot(pick, source, preferred_element_type=F32)
    out_ref[...] = packed.astype(BF16)


def pack_logs(logs):
    high = logs.astype(BF16).astype(F32)
    mid = (logs - high).astype(BF16).astype(F32)
    low = (logs - high - mid).astype(BF16).astype(F32)
    return (high + pltpu.roll(mid, LOG_LANES, 1) + pltpu.roll(low, 2 * LOG_LANES, 1)).astype(BF16)


def unpack_logs(packed):
    kept = packed.astype(F32)
    return kept + pltpu.roll(kept, HD - LOG_LANES, 1) + pltpu.roll(kept, HD - 2 * LOG_LANES, 1)


def attention_kernel(plan, fetched, own, where_ref, *refs):
    *refs, out_ref, held_ref = refs
    line_refs, refs = refs[: plan.line], refs[plan.line :]
    inv_root = 1.0 / HD**0.5
    line, quad = where_ref[0] // QUAD, where_ref[0] & (QUAD - 1)
    lane = lax.broadcasted_iota(jnp.int32, (TILE, HD), 1)
    laid = [jnp.zeros((TILE, HD), F32) for _ in range(plan.line)]
    for step, ref in enumerate(line_refs):
        held_ref[pl.ds(pl.multiple_of((line ^ step) * plan.rows, TILE), plan.rows), :] = ref[...]
    first = plan.own_heads * plan.tok
    for chunk in range(first // plan.rows, plan.line):
        low = max(first - chunk * plan.rows, 0)
        if low < plan.rows:
            out_ref[chunk, low : plan.rows, :] = jnp.zeros((plan.rows - low, HD), BF16)
    for i in range(plan.own_heads):
        query = held_ref[i * plan.tok : (i + 1) * plan.tok, :]
        pairs = []
        for j in range(fetched):
            columns = slice(i * HD, (i + 1) * HD)
            pairs.append((refs[2 * j][:, columns], refs[2 * j + 1][:, columns]))
        if own:
            k_ref, v_ref = refs[2 * fetched :]
            columns = pl.ds(pl.multiple_of(plan.head_at(i, quad) * HD, HD), HD)
            pairs.append((k_ref[:, columns], v_ref[:, columns]))
        scores = [
            lax.dot_general(query, key, LANES_BOTH, preferred_element_type=F32) * inv_root
            for key, _ in pairs
        ]
        peak = functools.reduce(jnp.maximum, [jnp.max(s, axis=1, keepdims=True) for s in scores])
        expos = [jnp.exp(s - peak) for s in scores]
        total = functools.reduce(jnp.add, [jnp.sum(e, axis=1, keepdims=True) for e in expos])
        block = functools.reduce(
            jnp.add,
            [
                jnp.dot(e.astype(BF16), value, preferred_element_type=F32)
                for e, (_, value) in zip(expos, pairs)
            ],
        )
        block = (block / total).astype(BF16)
        logs = peak + jnp.log(total)
        for tile in range(plan.tok // TILE):
            chunk, place = divmod(i * (plan.tok // TILE) + tile, plan.tiles)
            mine = slice(tile * TILE, (tile + 1) * TILE)
            out_ref[chunk, place * TILE : (place + 1) * TILE, :] = block[mine]
            laid[chunk] = jnp.where(lane == place, logs[mine], laid[chunk])
    for chunk in range(plan.line):
        out_ref[chunk, plan.rows :, :] = pack_logs(laid[chunk])


def merge(plan, parts, out_ref, keep_logs):
    rows = plan.rows
    logs = [unpack_logs(part[rows:, :]) for part in parts]
    top = functools.reduce(jnp.maximum, logs)
    weights = [jnp.exp(log - top) for log in logs]
    total = functools.reduce(jnp.add, weights)
    scale = 1.0 / total
    weights = [weight * scale for weight in weights]
    for tile in range(plan.tiles):
        mine = slice(tile * TILE, (tile + 1) * TILE)
        mixed = functools.reduce(
            jnp.add,
            [w[:, tile : tile + 1] * part[mine, :].astype(F32) for w, part in zip(weights, parts)],
        )
        out_ref[mine, :] = mixed.astype(BF16)
    if keep_logs:
        lane = lax.broadcasted_iota(jnp.int32, (TILE, HD), 1)
        out_ref[rows:, :] = pack_logs(jnp.where(lane < LOG_LANES, top + jnp.log(total), 0.0))


def split_kernel(plan, where_ref, *refs):
    parts, outs = refs[: -plan.line], refs[-plan.line :]
    line = where_ref[0] // QUAD
    for step, out_ref in enumerate(outs):
        merge(plan, [part.at[line ^ step] for part in parts], out_ref, True)


def finish_kernel(plan, where_ref, near_ref, *refs):
    *refs, part_ref, held_ref = refs
    attention_kernel(plan, 2, False, where_ref, *refs[: -plan.line], part_ref, held_ref)
    split_kernel(plan, where_ref, near_ref, part_ref, *refs[-plan.line :])


def line_kernel(plan, *refs):
    merge(plan, refs[:-1], refs[-1], False)


def stack_kernel(plan, where_ref, *refs):
    *parts, low_ref, high_ref, held_ref = refs
    line = where_ref[0] // QUAD
    for step, part in enumerate(parts):
        held_ref[line ^ step] = part[...]
    for i in range(plan.line // 2):
        low_ref[i * plan.rows : (i + 1) * plan.rows, :] = held_ref[i]
        high_ref[i * plan.rows : (i + 1) * plan.rows, :] = held_ref[plan.line // 2 + i]


def project_group(plan, quad, refs, w_ref):
    sides, weights = [], []
    for i in range(plan.own_heads):
        block = plan.head_rows(refs, i)
        if plan.own_heads * QUAD != plan.heads:
            block = jnp.where(i * QUAD + quad < plan.heads, block, jnp.zeros_like(block))
        sides.append(block)
        columns = pl.ds(pl.multiple_of(plan.head_at(i, quad) * HD, HD), HD)
        weights.append(w_ref[:, columns])
    return lax.dot_general(
        jnp.concatenate(sides, axis=1),
        jnp.concatenate(weights, axis=1),
        LANES_BOTH,
        preferred_element_type=F32,
    )


def project_kernel(plan, steps, where_ref, w_ref, *refs):
    *refs, out_ref = refs
    total = None
    if len(refs) % 2:
        *refs, sum_ref = refs
        total = sum_ref[...]
    for i, step in enumerate(steps):
        quad = (where_ref[0] & (QUAD - 1)) ^ step
        term = project_group(plan, quad, refs[2 * i : 2 * i + 2], w_ref)
        total = term if total is None else total + term
    out_ref[...] = total


def place_kernel(plan, step, where_ref, w_ref, low_ref, high_ref, sum_ref, info_ref, out_ref):
    devices, cap, tok = plan.devices, plan.cap, plan.tok
    quad = (where_ref[0] & (QUAD - 1)) ^ step
    proj = sum_ref[...] + project_group(plan, quad, (low_ref, high_ref), w_ref)
    picks = []
    for device in range(devices):
        place = iota((cap, tok), 0)
        count = info_ref[0, device : device + 1, 0:1]
        offset = info_ref[1, device : device + 1, 0:1]
        picks.append(
            ((iota((cap, tok), 1) - offset == place) & (place < count)).astype(F32).astype(BF16)
        )
    pick = jnp.concatenate(picks, axis=0)
    laid = jnp.dot(pick, proj.astype(BF16), preferred_element_type=F32).astype(BF16)
    out_ref[...] = laid.reshape(devices, cap, w_ref.shape[0])


def update_kernel(plan, halves, half_ref, act_ref, *refs):
    *term_refs, hidden_ref, cached_ref, out_hbm, held_ref, sems = refs
    cap, width = plan.cap, term_refs[0].shape[-1]
    wide = math.lcm(width, HD)
    blocks, steps = wide // width, hidden_ref.shape[1] // wide
    chosen = own_selection(act_ref[...].astype(F32), cap)
    mask = lax.dot_general(chosen, jnp.ones((cap, HD), BF16), ROWS_BOTH, preferred_element_type=F32)
    active = mask[:, 0:1] > 0
    copies = []
    for step in range(steps):
        terms = []
        for ref in term_refs:
            if ref.ndim == 3:
                first = half_ref[0] * (plan.devices // halves) + step * blocks
                sides = [[ref[first + j] for j in range(blocks)]]
            else:
                sides = [[ref[i, step * blocks + j] for j in range(blocks)] for i in range(halves)]
            for side in sides:
                terms.append(jnp.concatenate([b.astype(F32) for b in side], axis=1).astype(BF16))
        summed = lax.dot_general(
            jnp.concatenate([chosen] * len(terms), axis=0),
            jnp.concatenate(terms, axis=0),
            ROWS_BOTH,
            preferred_element_type=F32,
        )
        columns = slice(step * wide, (step + 1) * wide)
        updated = (hidden_ref[:, columns].astype(F32) + summed).astype(BF16)
        held_ref[:, columns] = jnp.where(active, updated, cached_ref[:, columns])
        copy = pltpu.make_async_copy(held_ref.at[:, columns], out_hbm.at[:, columns], sems.at[step])
        copy.start()
        copies.append(copy)
    for copy in copies:
        copy.wait()


def shape(*dims, dtype=BF16):
    return jax.ShapeDtypeStruct(dims, dtype)


def call(kernel, out_shape, *args, cost=None, hbm=(), out_hbm=(), grant=32, **options):
    def spec(i, arg):
        if i in hbm:
            return HBM
        return SMEM if arg.dtype == jnp.int32 and arg.ndim == 1 else VMEM

    return pl.pallas_call(
        kernel,
        out_shape=out_shape,
        in_specs=[spec(i, arg) for i, arg in enumerate(args)],
        out_specs=jax.tree.unflatten(
            jax.tree.structure(out_shape),
            [HBM if i in out_hbm else VMEM for i in range(len(jax.tree.leaves(out_shape)))],
        ),
        compiler_params=pltpu.CompilerParams(vmem_limit_bytes=grant << 20),
        cost_estimate=cost,
        **options,
    )(*args)


def exchange(value):
    return lax.all_to_all(value, "seq", split_axis=0, concat_axis=0, tiled=True)


def shift(value, mask):
    pairs = [(i, i ^ mask) for i in range(lax.axis_size("seq"))]
    return lax.ppermute(value, "seq", pairs)


def line_gather(plan, chunk):
    return [shift(chunk, step * QUAD) if step else chunk for step in range(plan.line)]


def quad_gather(low, high):
    x_low, y_high = shift(low, 1), shift(high, 2)
    x_high, y_low = shift(high, 1), shift(low, 2)
    return [(low, high), (x_low, x_high), (y_low, y_high), (shift(x_low, 2), shift(y_high, 1))]


def shards(queries, keys, values, hidden, cached, active, w_out):
    tok_dev, features = queries.shape
    devices, halves = lax.axis_size("seq"), lax.axis_size("head")
    plan = Plan(devices, tok_dev, features)
    cap, columns = plan.cap, w_out.shape[1]
    act = active.reshape(1, tok_dev)
    me = lax.axis_index("seq").astype(jnp.int32).reshape(1)
    dma = pltpu.SemaphoreType.DMA
    partial = functools.partial

    parts = math.gcd(features // HD, 5)
    wanted = ((0, 1), (0, 2), (1, 1), (1, 2), (0, 3), (1, 3))
    blocks = plan.own_heads * len(wanted)
    sent, *near_k, x_v, y_v, far_k, far_v = call(
        partial(prepare_kernel, plan, parts, wanted),
        (
            shape(devices, plan.spans * cap + 8, HD),
            *[shape(tok_dev, plan.own_heads * HD) for _ in wanted],
        ),
        act, queries, keys, values, hbm=range(4), out_hbm=range(1, 1 + len(wanted)), grant=56,
        scratch_shapes=[
            pltpu.VMEM((1, tok_dev), jnp.int32),
            pltpu.VMEM((tok_dev, features), BF16),
            pltpu.VMEM((cap, features), BF16),
            pltpu.VMEM((blocks, tok_dev, HD), BF16),
            dma((parts + 1,)), dma((blocks,)), dma((blocks,)),
        ],
    )
    near_k = [shift(part, i + 1) for i, part in enumerate(near_k)]
    spread = exchange(sent)
    near_v = [shift(x_v, 1), shift(y_v, 2)]
    far = [shift(far_k, 3), shift(far_v, 3)]
    near, far = [near_k[0], near_v[0]], [near_k[1], near_v[1], *far]
    chunk, info = call(
        partial(compact_kernel, plan),
        (shape(plan.rows, HD), shape(2, devices, HD, dtype=F32)), me, spread,
    )
    line = line_gather(plan, chunk)
    scored = plan.own_heads * plan.tok * tok_dev

    def attend(kernel, count, out, *args, **options):
        cost = pl.CostEstimate(
            flops=4 * count * scored * HD,
            transcendentals=count * scored,
            bytes_accessed=4 * count * tok_dev * HD * plan.own_heads,
        )
        held = pltpu.VMEM((plan.line * plan.rows, HD), BF16)
        scratch = [*options.get("scratch", ()), held]
        return call(kernel, out, me, *args, cost=cost, scratch_shapes=scratch)

    scored_shape = (plan.line, plan.rows + TILE, HD)
    part = attend(
        partial(attention_kernel, plan, 1, True), 2,
        shape(*scored_shape), *line, *near, keys, values,
    )
    sums = attend(
        partial(finish_kernel, plan), 2,
        tuple(shape(plan.rows + TILE, HD) for _ in range(plan.line)),
        part, *line, *far, scratch=[pltpu.VMEM(scored_shape, BF16)],
    )
    arrived = [shift(part, step * QUAD) if step else part for step, part in enumerate(sums)]
    chunk = call(partial(line_kernel, plan), shape(plan.rows, HD), *arrived)
    low, high = call(
        partial(stack_kernel, plan), (shape(plan.half, HD), shape(plan.half, HD)),
        me, *line_gather(plan, chunk),
        scratch_shapes=[pltpu.VMEM((plan.line, plan.rows, HD), BF16)],
    )
    w_rows = w_out.T
    cost = pl.CostEstimate(
        flops=2 * plan.own_heads * plan.tok * HD * columns,
        transcendentals=0,
        bytes_accessed=2 * plan.own_heads * HD * columns,
    )
    groups = quad_gather(low, high)
    proj = None
    for step in range(QUAD - 1):
        extra = () if proj is None else (proj,)
        proj = call(
            partial(project_kernel, plan, (step,)),
            shape(plan.tok, columns, dtype=F32), me, w_rows, *groups[step], *extra, cost=cost,
        )
    terms = call(
        partial(place_kernel, plan, QUAD - 1),
        shape(devices, cap, columns), me, w_rows, *groups[QUAD - 1], proj, info,
    )
    arrived = exchange(terms)

    half = lax.axis_index("head").astype(jnp.int32).reshape(1)
    if halves == 2:
        term_args = [arrived, lax.ppermute(arrived, "head", [(0, 1), (1, 0)])]
    else:
        split = arrived.reshape(halves, devices // halves, cap, columns)
        term_args = [lax.all_to_all(split, "head", split_axis=0, concat_axis=0, tiled=True)]
    return call(
        partial(update_kernel, plan, halves),
        shape(tok_dev, features), half, act, *term_args, hidden, cached, out_hbm=(0,),
        scratch_shapes=[
            pltpu.VMEM((tok_dev, features), BF16),
            dma((features // math.lcm(columns, HD),)),
        ],
    )


def solution(mesh):
    placed = (
        P("seq", "head"),
        P("seq", "head"),
        P("seq", "head"),
        P("seq", "head"),
        P("seq", "head"),
        P("seq"),
        P("head", "seq"),
    )


    return jax.shard_map(
        shards, mesh=mesh, in_specs=placed, out_specs=P("seq", "head"), check_vma=False
    )
```

```python
import functools
import math

import jax
import jax.numpy as jnp
from jax import lax
from jax.experimental import pallas as pl
from jax.experimental.pallas import tpu as pltpu
from jax.sharding import PartitionSpec as P


HD = 128
TILE = 16
QUAD = 4
LOG_LANES = 32
F32 = jnp.float32
BF16 = jnp.bfloat16
VMEM = pl.BlockSpec(memory_space=pltpu.VMEM)
SMEM = pl.BlockSpec(memory_space=pltpu.SMEM)
HBM = pl.BlockSpec(memory_space=pltpu.HBM)
LANES_BOTH = (((1,), (1,)), ((), ()))
ROWS_BOTH = (((0,), (0,)), ((), ()))


def iota(shape, dim):
    return lax.broadcasted_iota(jnp.int32, shape, dim).astype(F32)


class Plan:
    def __init__(self, devices, tok_dev, features):
        assert devices % (2 * QUAD) == 0
        self.devices = devices
        self.line = devices // QUAD
        self.heads = features // HD
        self.own_heads = -(-self.heads // QUAD)
        self.cap = tok_dev // 8
        self.total = devices * tok_dev * 11 // 256
        groups = -(-self.total // TILE)
        self.tok = groups * TILE
        self.tiles = -(-self.own_heads * groups // self.line)
        self.rows = self.tiles * TILE
        self.half = self.line // 2 * self.rows
        self.spans = max(
            min((self.tiles * (line + 1) - 1) // groups, self.own_heads - 1) - self.tiles * line // groups + 1
            for line in range(self.line)
        )
        assert self.tiles <= LOG_LANES

    def head_at(self, index, quad):
        return jnp.minimum(index * QUAD + quad, self.heads - 1)

    def first_head(self, line):
        return line * self.tiles * TILE // self.tok

    def sent_heads(self, device):
        first = self.first_head(device // QUAD)
        local = [min(first + i, self.own_heads - 1) for i in range(self.spans)]
        return [min(i * QUAD + device % QUAD, self.heads - 1) for i in local]

    def head_rows(self, refs, index):
        first, last = index * self.tok, (index + 1) * self.tok
        parts = []
        for i, ref in enumerate(refs):
            low, high = max(first - i * self.half, 0), min(last - i * self.half, self.half)
            if low < high:
                parts.append(ref[low:high, :])
        return parts[0] if len(parts) == 1 else jnp.concatenate(parts, axis=0)


def own_selection(act, cap):
    tokens = act.shape[1]
    before = (iota((tokens, tokens), 0) < iota((tokens, tokens), 1)).astype(BF16)
    many = jnp.broadcast_to(act, (TILE, tokens)).astype(BF16)
    rank = jnp.dot(many, before, preferred_element_type=F32)[0:1]
    rank = jnp.where(act > 0, rank, -1.0)
    return (iota((cap, tokens), 0) == rank).astype(BF16)


def prepare_kernel(plan, parts, wanted, act_hbm, q_hbm, k_hbm, v_hbm, *refs):
    out_ref, *fetched = refs[: 1 + len(wanted)]
    act_ref, q_ref, own_ref, passing, q_sems, in_sems, out_sems = refs[1 + len(wanted) :]
    me = lax.axis_index("seq")
    heads = plan.own_heads
    arriving, leaving = [], []
    for j, (source, step) in enumerate(wanted):
        quad = lax.rem(me, QUAD) ^ step
        for i in range(heads):
            columns = pl.ds(pl.multiple_of(plan.head_at(i, quad) * HD, HD), HD)
            n = j * heads + i
            taken = (k_hbm, v_hbm)[source].at[:, columns]
            target = fetched[j].at[:, i * HD : (i + 1) * HD]
            arriving.append(pltpu.make_async_copy(taken, passing.at[n], in_sems.at[n]))
            leaving.append(pltpu.make_async_copy(passing.at[n], target, out_sems.at[n]))
    wide = q_hbm.shape[1] // parts
    columns = [slice(i * wide, (i + 1) * wide) for i in range(parts)]
    queries = [
        pltpu.make_async_copy(q_hbm.at[:, c], q_ref.at[:, c], q_sems.at[i])
        for i, c in enumerate(columns)
    ]
    first = pltpu.make_async_copy(act_hbm, act_ref, q_sems.at[parts])
    early = 2 * heads
    for copy in [first, *arriving[:early], *queries, *arriving[early:]]:
        copy.start()

    def forward(low, high):
        for one, two in zip(arriving[low:high], leaving[low:high]):
            one.wait()
            two.start()

    first.wait()
    act = act_ref[...].astype(F32)
    chosen = own_selection(act, plan.cap)
    count = jnp.broadcast_to(jnp.sum(act, axis=1, keepdims=True), (8, HD)).astype(BF16)
    forward(0, early)
    for copy, c in zip(queries, columns):
        copy.wait()
        own_ref[:, c] = jnp.dot(chosen, q_ref[:, c], preferred_element_type=F32).astype(BF16)
    forward(early, len(arriving))
    for device in range(plan.devices):
        for i, head in enumerate(plan.sent_heads(device)):
            out_ref[device, i * plan.cap : (i + 1) * plan.cap, :] = own_ref[:, head * HD : (head + 1) * HD]
        out_ref[device, plan.spans * plan.cap :, :] = count
    for copy in leaving:
        copy.wait()


def compact_kernel(plan, where_ref, in_ref, out_ref, info_ref):
    devices, cap = plan.devices, plan.cap
    count = jnp.max(in_ref[:, plan.spans * cap :, :].astype(F32), axis=1)
    earlier = (iota((devices, devices), 1) < iota((devices, devices), 0)).astype(BF16)
    offset = jnp.dot(earlier, count.astype(BF16), preferred_element_type=F32)
    info_ref[0] = count
    info_ref[1] = offset
    slots = devices * cap
    place = iota((devices, slots), 1) - iota((devices, slots), 0) * cap
    held = (place >= 0) & (place < jnp.minimum(count[:, 0:1], float(cap)))
    ranks = jnp.sum(jnp.where(held, offset[:, 0:1] + place + 1.0, 0.0), axis=0, keepdims=True) - 1.0
    ranks = jnp.where(ranks < 0, -1.0e6, ranks)
    line = where_ref[0] // QUAD
    start = line * plan.rows - plan.first_head(line) * plan.tok
    packed = jnp.zeros((plan.rows, HD), F32)
    for i in range(plan.spans):
        token = iota((plan.rows, slots), 0) + (start - i * plan.tok).astype(F32)
        pick = (token == ranks).astype(BF16)
        source = in_ref[:, i * cap : (i + 1) * cap, :].reshape(slots, HD)
        packed = packed + jnp.dot(pick, source, preferred_element_type=F32)
    out_ref[...] = packed.astype(BF16)


def pack_logs(logs):
    high = logs.astype(BF16).astype(F32)
    mid = (logs - high).astype(BF16).astype(F32)
    low = (logs - high - mid).astype(BF16).astype(F32)
    return (high + pltpu.roll(mid, LOG_LANES, 1) + pltpu.roll(low, 2 * LOG_LANES, 1)).astype(BF16)


def unpack_logs(packed):
    kept = packed.astype(F32)
    return kept + pltpu.roll(kept, HD - LOG_LANES, 1) + pltpu.roll(kept, HD - 2 * LOG_LANES, 1)


def attention_kernel(plan, fetched, own, where_ref, *refs):
    *refs, out_ref, held_ref = refs
    line_refs, refs = refs[: plan.line], refs[plan.line :]
    inv_root = 1.0 / HD**0.5
    line, quad = where_ref[0] // QUAD, where_ref[0] & (QUAD - 1)
    lane = lax.broadcasted_iota(jnp.int32, (TILE, HD), 1)
    laid = [jnp.zeros((TILE, HD), F32) for _ in range(plan.line)]
    for step, ref in enumerate(line_refs):
        held_ref[pl.ds(pl.multiple_of((line ^ step) * plan.rows, TILE), plan.rows), :] = ref[...]
    first = plan.own_heads * plan.tok
    for chunk in range(first // plan.rows, plan.line):
        low = max(first - chunk * plan.rows, 0)
        if low < plan.rows:
            out_ref[chunk, low : plan.rows, :] = jnp.zeros((plan.rows - low, HD), BF16)
    for i in range(plan.own_heads):
        query = held_ref[i * plan.tok : (i + 1) * plan.tok, :]
        pairs = []
        for j in range(fetched):
            columns = slice(i * HD, (i + 1) * HD)
            pairs.append((refs[2 * j][:, columns], refs[2 * j + 1][:, columns]))
        if own:
            k_ref, v_ref = refs[2 * fetched :]
            columns = pl.ds(pl.multiple_of(plan.head_at(i, quad) * HD, HD), HD)
            pairs.append((k_ref[:, columns], v_ref[:, columns]))
        scores = [
            lax.dot_general(query, key, LANES_BOTH, preferred_element_type=F32) * inv_root
            for key, _ in pairs
        ]
        peak = functools.reduce(jnp.maximum, [jnp.max(s, axis=1, keepdims=True) for s in scores])
        expos = [jnp.exp(s - peak) for s in scores]
        total = functools.reduce(jnp.add, [jnp.sum(e, axis=1, keepdims=True) for e in expos])
        block = functools.reduce(
            jnp.add,
            [
                jnp.dot(e.astype(BF16), value, preferred_element_type=F32)
                for e, (_, value) in zip(expos, pairs)
            ],
        )
        block = (block / total).astype(BF16)
        logs = peak + jnp.log(total)
        for tile in range(plan.tok // TILE):
            chunk, place = divmod(i * (plan.tok // TILE) + tile, plan.tiles)
            mine = slice(tile * TILE, (tile + 1) * TILE)
            out_ref[chunk, place * TILE : (place + 1) * TILE, :] = block[mine]
            laid[chunk] = jnp.where(lane == place, logs[mine], laid[chunk])
    for chunk in range(plan.line):
        out_ref[chunk, plan.rows :, :] = pack_logs(laid[chunk])


def merge(plan, parts, out_ref, keep_logs):
    rows = plan.rows
    logs = [unpack_logs(part[rows:, :]) for part in parts]
    top = functools.reduce(jnp.maximum, logs)
    weights = [jnp.exp(log - top) for log in logs]
    total = functools.reduce(jnp.add, weights)
    scale = 1.0 / total
    weights = [weight * scale for weight in weights]
    for tile in range(plan.tiles):
        mine = slice(tile * TILE, (tile + 1) * TILE)
        mixed = functools.reduce(
            jnp.add,
            [w[:, tile : tile + 1] * part[mine, :].astype(F32) for w, part in zip(weights, parts)],
        )
        out_ref[mine, :] = mixed.astype(BF16)
    if keep_logs:
        lane = lax.broadcasted_iota(jnp.int32, (TILE, HD), 1)
        out_ref[rows:, :] = pack_logs(jnp.where(lane < LOG_LANES, top + jnp.log(total), 0.0))


def split_kernel(plan, where_ref, *refs):
    parts, outs = refs[: -plan.line], refs[-plan.line :]
    line = where_ref[0] // QUAD
    for step, out_ref in enumerate(outs):
        merge(plan, [part.at[line ^ step] for part in parts], out_ref, True)


def finish_kernel(plan, where_ref, near_ref, *refs):
    *refs, part_ref, held_ref = refs
    attention_kernel(plan, 2, False, where_ref, *refs[: -plan.line], part_ref, held_ref)
    split_kernel(plan, where_ref, near_ref, part_ref, *refs[-plan.line :])


def line_kernel(plan, *refs):
    merge(plan, refs[:-1], refs[-1], False)


def stack_kernel(plan, where_ref, *refs):
    *parts, low_ref, high_ref, held_ref = refs
    line = where_ref[0] // QUAD
    for step, part in enumerate(parts):
        held_ref[line ^ step] = part[...]
    for i in range(plan.line // 2):
        low_ref[i * plan.rows : (i + 1) * plan.rows, :] = held_ref[i]
        high_ref[i * plan.rows : (i + 1) * plan.rows, :] = held_ref[plan.line // 2 + i]


def project_group(plan, quad, refs, w_ref):
    sides, weights = [], []
    for i in range(plan.own_heads):
        block = plan.head_rows(refs, i)
        if plan.own_heads * QUAD != plan.heads:
            block = jnp.where(i * QUAD + quad < plan.heads, block, jnp.zeros_like(block))
        sides.append(block)
        columns = pl.ds(pl.multiple_of(plan.head_at(i, quad) * HD, HD), HD)
        weights.append(w_ref[:, columns])
    return lax.dot_general(
        jnp.concatenate(sides, axis=1),
        jnp.concatenate(weights, axis=1),
        LANES_BOTH,
        preferred_element_type=F32,
    )


def project_kernel(plan, steps, where_ref, w_ref, *refs):
    *refs, out_ref = refs
    total = None
    if len(refs) % 2:
        *refs, sum_ref = refs
        total = sum_ref[...]
    for i, step in enumerate(steps):
        quad = (where_ref[0] & (QUAD - 1)) ^ step
        term = project_group(plan, quad, refs[2 * i : 2 * i + 2], w_ref)
        total = term if total is None else total + term
    out_ref[...] = total


def place_kernel(plan, step, where_ref, w_ref, low_ref, high_ref, sum_ref, info_ref, out_ref):
    devices, cap, tok = plan.devices, plan.cap, plan.tok
    quad = (where_ref[0] & (QUAD - 1)) ^ step
    proj = sum_ref[...] + project_group(plan, quad, (low_ref, high_ref), w_ref)
    picks = []
    for device in range(devices):
        place = iota((cap, tok), 0)
        count = info_ref[0, device : device + 1, 0:1]
        offset = info_ref[1, device : device + 1, 0:1]
        picks.append(
            ((iota((cap, tok), 1) - offset == place) & (place < count)).astype(F32).astype(BF16)
        )
    pick = jnp.concatenate(picks, axis=0)
    laid = jnp.dot(pick, proj.astype(BF16), preferred_element_type=F32)
    for device in range(devices):
        rows = laid[device * cap : (device + 1) * cap]
        out_ref[device] = pack_rows(rows, cap, w_ref.shape[0]).astype(BF16)


def update_kernel(plan, halves, half_ref, act_ref, *refs):
    *term_refs, hidden_ref, cached_ref, out_hbm, held_ref, sems = refs
    cap, width = plan.cap, hidden_ref.shape[1] * halves // plan.devices
    wide = math.lcm(width, HD)
    blocks, steps = wide // width, hidden_ref.shape[1] // wide
    chosen = own_selection(act_ref[...].astype(F32), cap)
    mask = lax.dot_general(chosen, jnp.ones((cap, HD), BF16), ROWS_BOTH, preferred_element_type=F32)
    active = mask[:, 0:1] > 0
    copies = []
    for step in range(steps):
        terms = []
        for ref in term_refs:
            if ref.ndim == 3:
                first = half_ref[0] * (plan.devices // halves) + step * blocks
                sides = [[ref[first + j] for j in range(blocks)]]
            else:
                sides = [[ref[i, step * blocks + j] for j in range(blocks)] for i in range(halves)]
            for side in sides:
                wide_rows = [c for b in side for c in unpack_rows(b.astype(F32), cap, width)]
                terms.append(jnp.concatenate(wide_rows, axis=1).astype(BF16))
        summed = lax.dot_general(
            jnp.concatenate([chosen] * len(terms), axis=0),
            jnp.concatenate(terms, axis=0),
            ROWS_BOTH,
            preferred_element_type=F32,
        )
        columns = slice(step * wide, (step + 1) * wide)
        updated = (hidden_ref[:, columns].astype(F32) + summed).astype(BF16)
        held_ref[:, columns] = jnp.where(active, updated, cached_ref[:, columns])
        copy = pltpu.make_async_copy(held_ref.at[:, columns], out_hbm.at[:, columns], sems.at[step])
        copy.start()
        copies.append(copy)
    for copy in copies:
        copy.wait()


def packing(cap, width):
    whole, rest = divmod(width, HD)
    blocks = [(i * cap, 0, cap, i * HD, 0, HD) for i in range(whole)]
    if rest and HD % rest == 0 and cap % (HD // rest * TILE) == 0:
        fold = cap * rest // HD
        blocks += [(whole * cap, i * fold, fold, whole * HD, i * rest, rest) for i in range(HD // rest)]
        return whole * cap + fold, blocks
    if rest:
        blocks.append((whole * cap, 0, cap, whole * HD, 0, rest))
    return (whole + (1 if rest else 0)) * cap, blocks


def pack_rows(rows, cap, width):
    _, blocks = packing(cap, width)
    pieces = {}
    for first, row, count, column, lane, columns in blocks:
        pieces.setdefault(first, []).append(rows[row : row + count, column : column + columns])
    joined = []
    for first in sorted(pieces):
        side = jnp.concatenate(pieces[first], axis=1) if len(pieces[first]) > 1 else pieces[first][0]
        if side.shape[1] < HD:
            side = jnp.concatenate([side, jnp.zeros((side.shape[0], HD - side.shape[1]), side.dtype)], axis=1)
        joined.append(side)
    return jnp.concatenate(joined, axis=0)


def unpack_rows(packed, cap, width):
    _, blocks = packing(cap, width)
    columns = {}
    for first, row, count, column, lane, wide in blocks:
        columns.setdefault(column, []).append(packed[first : first + count, lane : lane + wide])
    return [jnp.concatenate(columns[c], axis=0) for c in sorted(columns)]


def shape(*dims, dtype=BF16):
    return jax.ShapeDtypeStruct(dims, dtype)


def call(kernel, out_shape, *args, cost=None, hbm=(), out_hbm=(), grant=32, **options):
    def spec(i, arg):
        if i in hbm:
            return HBM
        return SMEM if arg.dtype == jnp.int32 and arg.ndim == 1 else VMEM

    return pl.pallas_call(
        kernel,
        out_shape=out_shape,
        in_specs=[spec(i, arg) for i, arg in enumerate(args)],
        out_specs=jax.tree.unflatten(
            jax.tree.structure(out_shape),
            [HBM if i in out_hbm else VMEM for i in range(len(jax.tree.leaves(out_shape)))],
        ),
        compiler_params=pltpu.CompilerParams(vmem_limit_bytes=grant << 20),
        cost_estimate=cost,
        **options,
    )(*args)


def exchange(value):
    return lax.all_to_all(value, "seq", split_axis=0, concat_axis=0, tiled=True)


def shift(value, mask):
    pairs = [(i, i ^ mask) for i in range(lax.axis_size("seq"))]
    return lax.ppermute(value, "seq", pairs)


def line_gather(plan, chunk):
    return [shift(chunk, step * QUAD) if step else chunk for step in range(plan.line)]


def quad_gather(low, high):
    x_low, y_high = shift(low, 1), shift(high, 2)
    x_high, y_low = shift(high, 1), shift(low, 2)
    return [(low, high), (x_low, x_high), (y_low, y_high), (shift(x_low, 2), shift(y_high, 1))]


def shards(queries, keys, values, hidden, cached, active, w_out):
    tok_dev, features = queries.shape
    devices, halves = lax.axis_size("seq"), lax.axis_size("head")
    plan = Plan(devices, tok_dev, features)
    cap, columns = plan.cap, w_out.shape[1]
    act = active.reshape(1, tok_dev)
    me = lax.axis_index("seq").astype(jnp.int32).reshape(1)
    dma = pltpu.SemaphoreType.DMA
    partial = functools.partial

    parts = math.gcd(features // HD, 5)
    wanted = ((0, 1), (0, 2), (1, 1), (1, 2), (0, 3), (1, 3))
    blocks = plan.own_heads * len(wanted)
    sent, *near_k, x_v, y_v, far_k, far_v = call(
        partial(prepare_kernel, plan, parts, wanted),
        (
            shape(devices, plan.spans * cap + 8, HD),
            *[shape(tok_dev, plan.own_heads * HD) for _ in wanted],
        ),
        act, queries, keys, values, hbm=range(4), out_hbm=range(1, 1 + len(wanted)), grant=56,
        scratch_shapes=[
            pltpu.VMEM((1, tok_dev), jnp.int32),
            pltpu.VMEM((tok_dev, features), BF16),
            pltpu.VMEM((cap, features), BF16),
            pltpu.VMEM((blocks, tok_dev, HD), BF16),
            dma((parts + 1,)), dma((blocks,)), dma((blocks,)),
        ],
    )
    near_k = [shift(part, i + 1) for i, part in enumerate(near_k)]
    spread = exchange(sent)
    near_v = [shift(x_v, 1), shift(y_v, 2)]
    far = [shift(far_k, 3), shift(far_v, 3)]
    near, far = [near_k[0], near_v[0]], [near_k[1], near_v[1], *far]
    chunk, info = call(
        partial(compact_kernel, plan),
        (shape(plan.rows, HD), shape(2, devices, HD, dtype=F32)), me, spread,
    )
    line = line_gather(plan, chunk)
    scored = plan.own_heads * plan.tok * tok_dev

    def attend(kernel, count, out, *args, **options):
        cost = pl.CostEstimate(
            flops=4 * count * scored * HD,
            transcendentals=count * scored,
            bytes_accessed=4 * count * tok_dev * HD * plan.own_heads,
        )
        held = pltpu.VMEM((plan.line * plan.rows, HD), BF16)
        scratch = [*options.get("scratch", ()), held]
        return call(kernel, out, me, *args, cost=cost, scratch_shapes=scratch)

    scored_shape = (plan.line, plan.rows + TILE, HD)
    part = attend(
        partial(attention_kernel, plan, 1, True), 2,
        shape(*scored_shape), *line, *near, keys, values,
    )
    sums = attend(
        partial(finish_kernel, plan), 2,
        tuple(shape(plan.rows + TILE, HD) for _ in range(plan.line)),
        part, *line, *far, scratch=[pltpu.VMEM(scored_shape, BF16)],
    )
    arrived = [shift(part, step * QUAD) if step else part for step, part in enumerate(sums)]
    chunk = call(partial(line_kernel, plan), shape(plan.rows, HD), *arrived)
    low, high = call(
        partial(stack_kernel, plan), (shape(plan.half, HD), shape(plan.half, HD)),
        me, *line_gather(plan, chunk),
        scratch_shapes=[pltpu.VMEM((plan.line, plan.rows, HD), BF16)],
    )
    w_rows = w_out.T
    cost = pl.CostEstimate(
        flops=2 * plan.own_heads * plan.tok * HD * columns,
        transcendentals=0,
        bytes_accessed=2 * plan.own_heads * HD * columns,
    )
    groups = quad_gather(low, high)
    proj = None
    for step in range(QUAD - 1):
        extra = () if proj is None else (proj,)
        proj = call(
            partial(project_kernel, plan, (step,)),
            shape(plan.tok, columns, dtype=F32), me, w_rows, *groups[step], *extra, cost=cost,
        )
    terms = call(
        partial(place_kernel, plan, QUAD - 1),
        shape(devices, packing(cap, columns)[0], HD), me, w_rows, *groups[QUAD - 1], proj, info,
    )
    arrived = exchange(terms)

    half = lax.axis_index("head").astype(jnp.int32).reshape(1)
    if halves == 2:
        term_args = [arrived, lax.ppermute(arrived, "head", [(0, 1), (1, 0)])]
    else:
        split = arrived.reshape(halves, devices // halves, *arrived.shape[1:])
        term_args = [lax.all_to_all(split, "head", split_axis=0, concat_axis=0, tiled=True)]
    return call(
        partial(update_kernel, plan, halves),
        shape(tok_dev, features), half, act, *term_args, hidden, cached, out_hbm=(0,),
        scratch_shapes=[
            pltpu.VMEM((tok_dev, features), BF16),
            dma((features // math.lcm(columns, HD),)),
        ],
    )


def solution(mesh):
    placed = (
        P("seq", "head"),
        P("seq", "head"),
        P("seq", "head"),
        P("seq", "head"),
        P("seq", "head"),
        P("seq"),
        P("head", "seq"),
    )


    return jax.shard_map(
        shards, mesh=mesh, in_specs=placed, out_specs=P("seq", "head"), check_vma=False
    )
```

```python
import functools
import math

import jax
import jax.numpy as jnp
from jax import lax
from jax.experimental import pallas as pl
from jax.experimental.pallas import tpu as pltpu
from jax.sharding import PartitionSpec as P


HD = 128
TILE = 16
QUAD = 4
LOG_LANES = 32
F32 = jnp.float32
BF16 = jnp.bfloat16
VMEM = pl.BlockSpec(memory_space=pltpu.VMEM)
SMEM = pl.BlockSpec(memory_space=pltpu.SMEM)
HBM = pl.BlockSpec(memory_space=pltpu.HBM)
LANES_BOTH = (((1,), (1,)), ((), ()))
ROWS_BOTH = (((0,), (0,)), ((), ()))


def iota(shape, dim):
    return lax.broadcasted_iota(jnp.int32, shape, dim).astype(F32)


class Plan:
    def __init__(self, devices, tok_dev, features):
        assert devices % (2 * QUAD) == 0
        self.devices = devices
        self.line = devices // QUAD
        self.heads = features // HD
        self.own_heads = -(-self.heads // QUAD)
        self.cap = tok_dev // 8
        self.total = devices * tok_dev * 11 // 256
        groups = -(-self.total // TILE)
        self.tok = groups * TILE
        self.tiles = -(-self.own_heads * groups // self.line)
        self.rows = self.tiles * TILE
        self.half = self.line // 2 * self.rows
        self.spans = max(
            min((self.tiles * (line + 1) - 1) // groups, self.own_heads - 1) - self.tiles * line // groups + 1
            for line in range(self.line)
        )
        assert self.tiles <= LOG_LANES

    def head_at(self, index, quad):
        return jnp.minimum(index * QUAD + quad, self.heads - 1)

    def first_head(self, line):
        return line * self.tiles * TILE // self.tok

    def sent_heads(self, device):
        first = self.first_head(device // QUAD)
        local = [min(first + i, self.own_heads - 1) for i in range(self.spans)]
        return [min(i * QUAD + device % QUAD, self.heads - 1) for i in local]

    def head_rows(self, refs, index):
        first, last = index * self.tok, (index + 1) * self.tok
        parts = []
        for i, ref in enumerate(refs):
            low, high = max(first - i * self.half, 0), min(last - i * self.half, self.half)
            if low < high:
                parts.append(ref[low:high, :])
        return parts[0] if len(parts) == 1 else jnp.concatenate(parts, axis=0)


def own_selection(act, cap):
    tokens = act.shape[1]
    before = (iota((tokens, tokens), 0) < iota((tokens, tokens), 1)).astype(BF16)
    many = jnp.broadcast_to(act, (TILE, tokens)).astype(BF16)
    rank = jnp.dot(many, before, preferred_element_type=F32)[0:1]
    rank = jnp.where(act > 0, rank, -1.0)
    return (iota((cap, tokens), 0) == rank).astype(BF16)


def prepare_kernel(plan, parts, wanted, act_hbm, q_hbm, k_hbm, v_hbm, *refs):
    out_ref, *fetched = refs[: 1 + len(wanted)]
    act_ref, q_ref, own_ref, q_sems, in_sems = refs[1 + len(wanted) :]
    me = lax.axis_index("seq")
    heads = plan.own_heads
    arriving = []
    for (source, step), ref in zip(wanted, fetched):
        quad = lax.rem(me, QUAD) ^ step
        for i in range(heads):
            columns = pl.ds(pl.multiple_of(plan.head_at(i, quad) * HD, HD), HD)
            taken = (k_hbm, v_hbm)[source].at[:, columns]
            target = ref.at[:, i * HD : (i + 1) * HD]
            arriving.append(pltpu.make_async_copy(taken, target, in_sems.at[len(arriving)]))
    wide = q_hbm.shape[1] // parts
    columns = [slice(i * wide, (i + 1) * wide) for i in range(parts)]
    queries = [
        pltpu.make_async_copy(q_hbm.at[:, c], q_ref.at[:, c], q_sems.at[i])
        for i, c in enumerate(columns)
    ]
    first = pltpu.make_async_copy(act_hbm, act_ref, q_sems.at[parts])
    early = 2 * heads
    for copy in [first, *arriving[:early], *queries, *arriving[early:]]:
        copy.start()

    first.wait()
    act = act_ref[...].astype(F32)
    chosen = own_selection(act, plan.cap)
    count = jnp.broadcast_to(jnp.sum(act, axis=1, keepdims=True), (8, HD)).astype(BF16)
    for copy, c in zip(queries, columns):
        copy.wait()
        own_ref[:, c] = jnp.dot(chosen, q_ref[:, c], preferred_element_type=F32).astype(BF16)
    for device in range(plan.devices):
        for i, head in enumerate(plan.sent_heads(device)):
            out_ref[device, i * plan.cap : (i + 1) * plan.cap, :] = own_ref[:, head * HD : (head + 1) * HD]
        out_ref[device, plan.spans * plan.cap :, :] = count
    for copy in arriving:
        copy.wait()


def compact_kernel(plan, where_ref, in_ref, out_ref, info_ref):
    devices, cap = plan.devices, plan.cap
    count = jnp.max(in_ref[:, plan.spans * cap :, :].astype(F32), axis=1)
    earlier = (iota((devices, devices), 1) < iota((devices, devices), 0)).astype(BF16)
    offset = jnp.dot(earlier, count.astype(BF16), preferred_element_type=F32)
    info_ref[0] = count
    info_ref[1] = offset
    slots = devices * cap
    place = iota((devices, slots), 1) - iota((devices, slots), 0) * cap
    held = (place >= 0) & (place < jnp.minimum(count[:, 0:1], float(cap)))
    ranks = jnp.sum(jnp.where(held, offset[:, 0:1] + place + 1.0, 0.0), axis=0, keepdims=True) - 1.0
    ranks = jnp.where(ranks < 0, -1.0e6, ranks)
    line = where_ref[0] // QUAD
    start = line * plan.rows - plan.first_head(line) * plan.tok
    packed = jnp.zeros((plan.rows, HD), F32)
    for i in range(plan.spans):
        token = iota((plan.rows, slots), 0) + (start - i * plan.tok).astype(F32)
        pick = (token == ranks).astype(BF16)
        source = in_ref[:, i * cap : (i + 1) * cap, :].reshape(slots, HD)
        packed = packed + jnp.dot(pick, source, preferred_element_type=F32)
    out_ref[...] = packed.astype(BF16)


def pack_logs(logs):
    high = logs.astype(BF16).astype(F32)
    mid = (logs - high).astype(BF16).astype(F32)
    low = (logs - high - mid).astype(BF16).astype(F32)
    return (high + pltpu.roll(mid, LOG_LANES, 1) + pltpu.roll(low, 2 * LOG_LANES, 1)).astype(BF16)


def unpack_logs(packed):
    kept = packed.astype(F32)
    return kept + pltpu.roll(kept, HD - LOG_LANES, 1) + pltpu.roll(kept, HD - 2 * LOG_LANES, 1)


def attention_kernel(plan, fetched, own, where_ref, *refs):
    *refs, out_ref, held_ref = refs
    line_refs, refs = refs[: plan.line], refs[plan.line :]
    inv_root = 1.0 / HD**0.5
    line, quad = where_ref[0] // QUAD, where_ref[0] & (QUAD - 1)
    lane = lax.broadcasted_iota(jnp.int32, (TILE, HD), 1)
    laid = [jnp.zeros((TILE, HD), F32) for _ in range(plan.line)]
    for step, ref in enumerate(line_refs):
        held_ref[pl.ds(pl.multiple_of((line ^ step) * plan.rows, TILE), plan.rows), :] = ref[...]
    first = plan.own_heads * plan.tok
    for chunk in range(first // plan.rows, plan.line):
        low = max(first - chunk * plan.rows, 0)
        if low < plan.rows:
            out_ref[chunk, low : plan.rows, :] = jnp.zeros((plan.rows - low, HD), BF16)
    for i in range(plan.own_heads):
        query = held_ref[i * plan.tok : (i + 1) * plan.tok, :]
        pairs = []
        for j in range(fetched):
            columns = slice(i * HD, (i + 1) * HD)
            pairs.append((refs[2 * j][:, columns], refs[2 * j + 1][:, columns]))
        if own:
            k_ref, v_ref = refs[2 * fetched :]
            columns = pl.ds(pl.multiple_of(plan.head_at(i, quad) * HD, HD), HD)
            pairs.append((k_ref[:, columns], v_ref[:, columns]))
        scores = [
            lax.dot_general(query, key, LANES_BOTH, preferred_element_type=F32) * inv_root
            for key, _ in pairs
        ]
        peak = functools.reduce(jnp.maximum, [jnp.max(s, axis=1, keepdims=True) for s in scores])
        expos = [jnp.exp(s - peak) for s in scores]
        total = functools.reduce(jnp.add, [jnp.sum(e, axis=1, keepdims=True) for e in expos])
        block = functools.reduce(
            jnp.add,
            [
                jnp.dot(e.astype(BF16), value, preferred_element_type=F32)
                for e, (_, value) in zip(expos, pairs)
            ],
        )
        block = (block / total).astype(BF16)
        logs = peak + jnp.log(total)
        for tile in range(plan.tok // TILE):
            chunk, place = divmod(i * (plan.tok // TILE) + tile, plan.tiles)
            mine = slice(tile * TILE, (tile + 1) * TILE)
            out_ref[chunk, place * TILE : (place + 1) * TILE, :] = block[mine]
            laid[chunk] = jnp.where(lane == place, logs[mine], laid[chunk])
    for chunk in range(plan.line):
        out_ref[chunk, plan.rows :, :] = pack_logs(laid[chunk])


def merge(plan, parts, out_ref, keep_logs):
    rows = plan.rows
    logs = [unpack_logs(part[rows:, :]) for part in parts]
    top = functools.reduce(jnp.maximum, logs)
    weights = [jnp.exp(log - top) for log in logs]
    total = functools.reduce(jnp.add, weights)
    scale = 1.0 / total
    weights = [weight * scale for weight in weights]
    for tile in range(plan.tiles):
        mine = slice(tile * TILE, (tile + 1) * TILE)
        mixed = functools.reduce(
            jnp.add,
            [w[:, tile : tile + 1] * part[mine, :].astype(F32) for w, part in zip(weights, parts)],
        )
        out_ref[mine, :] = mixed.astype(BF16)
    if keep_logs:
        lane = lax.broadcasted_iota(jnp.int32, (TILE, HD), 1)
        out_ref[rows:, :] = pack_logs(jnp.where(lane < LOG_LANES, top + jnp.log(total), 0.0))


def split_kernel(plan, where_ref, *refs):
    parts, outs = refs[: -plan.line], refs[-plan.line :]
    line = where_ref[0] // QUAD
    for step, out_ref in enumerate(outs):
        merge(plan, [part.at[line ^ step] for part in parts], out_ref, True)


def finish_kernel(plan, where_ref, near_ref, *refs):
    *refs, part_ref, held_ref = refs
    attention_kernel(plan, 2, False, where_ref, *refs[: -plan.line], part_ref, held_ref)
    split_kernel(plan, where_ref, near_ref, part_ref, *refs[-plan.line :])


def line_kernel(plan, *refs):
    merge(plan, refs[:-1], refs[-1], False)


def stack_kernel(plan, where_ref, *refs):
    *parts, low_ref, high_ref, held_ref = refs
    line = where_ref[0] // QUAD
    for step, part in enumerate(parts):
        held_ref[line ^ step] = part[...]
    for i in range(plan.line // 2):
        low_ref[i * plan.rows : (i + 1) * plan.rows, :] = held_ref[i]
        high_ref[i * plan.rows : (i + 1) * plan.rows, :] = held_ref[plan.line // 2 + i]


def project_group(plan, quad, refs, w_ref):
    sides, weights = [], []
    for i in range(plan.own_heads):
        block = plan.head_rows(refs, i)
        if plan.own_heads * QUAD != plan.heads:
            block = jnp.where(i * QUAD + quad < plan.heads, block, jnp.zeros_like(block))
        sides.append(block)
        columns = pl.ds(pl.multiple_of(plan.head_at(i, quad) * HD, HD), HD)
        weights.append(w_ref[:, columns])
    return lax.dot_general(
        jnp.concatenate(sides, axis=1),
        jnp.concatenate(weights, axis=1),
        LANES_BOTH,
        preferred_element_type=F32,
    )


def project_kernel(plan, steps, where_ref, w_ref, *refs):
    *refs, out_ref = refs
    total = None
    if len(refs) % 2:
        *refs, sum_ref = refs
        total = sum_ref[...]
    for i, step in enumerate(steps):
        quad = (where_ref[0] & (QUAD - 1)) ^ step
        term = project_group(plan, quad, refs[2 * i : 2 * i + 2], w_ref)
        total = term if total is None else total + term
    out_ref[...] = total


def place_kernel(plan, step, where_ref, w_ref, low_ref, high_ref, sum_ref, info_ref, out_ref):
    devices, cap, tok = plan.devices, plan.cap, plan.tok
    quad = (where_ref[0] & (QUAD - 1)) ^ step
    proj = sum_ref[...] + project_group(plan, quad, (low_ref, high_ref), w_ref)
    picks = []
    for device in range(devices):
        place = iota((cap, tok), 0)
        count = info_ref[0, device : device + 1, 0:1]
        offset = info_ref[1, device : device + 1, 0:1]
        picks.append(
            ((iota((cap, tok), 1) - offset == place) & (place < count)).astype(F32).astype(BF16)
        )
    pick = jnp.concatenate(picks, axis=0)
    laid = jnp.dot(pick, proj.astype(BF16), preferred_element_type=F32)
    for device in range(devices):
        rows = laid[device * cap : (device + 1) * cap]
        out_ref[device] = pack_rows(rows, cap, w_ref.shape[0]).astype(BF16)


def update_kernel(plan, halves, half_ref, act_ref, *refs):
    *term_refs, hidden_ref, cached_ref, out_hbm, held_ref, sems = refs
    cap, width = plan.cap, hidden_ref.shape[1] * halves // plan.devices
    wide = math.lcm(width, HD)
    blocks, steps = wide // width, hidden_ref.shape[1] // wide
    chosen = own_selection(act_ref[...].astype(F32), cap)
    mask = lax.dot_general(chosen, jnp.ones((cap, HD), BF16), ROWS_BOTH, preferred_element_type=F32)
    active = mask[:, 0:1] > 0
    copies = []
    for step in range(steps):
        terms = []
        for ref in term_refs:
            if ref.ndim == 3:
                first = half_ref[0] * (plan.devices // halves) + step * blocks
                sides = [[ref[first + j] for j in range(blocks)]]
            else:
                sides = [[ref[i, step * blocks + j] for j in range(blocks)] for i in range(halves)]
            for side in sides:
                wide_rows = [c for b in side for c in unpack_rows(b.astype(F32), cap, width)]
                terms.append(jnp.concatenate(wide_rows, axis=1).astype(BF16))
        summed = lax.dot_general(
            jnp.concatenate([chosen] * len(terms), axis=0),
            jnp.concatenate(terms, axis=0),
            ROWS_BOTH,
            preferred_element_type=F32,
        )
        columns = slice(step * wide, (step + 1) * wide)
        updated = (hidden_ref[:, columns].astype(F32) + summed).astype(BF16)
        held_ref[:, columns] = jnp.where(active, updated, cached_ref[:, columns])
        copy = pltpu.make_async_copy(held_ref.at[:, columns], out_hbm.at[:, columns], sems.at[step])
        copy.start()
        copies.append(copy)
    for copy in copies:
        copy.wait()


def packing(cap, width):
    whole, rest = divmod(width, HD)
    blocks = [(i * cap, 0, cap, i * HD, 0, HD) for i in range(whole)]
    if rest and HD % rest == 0 and cap % (HD // rest * TILE) == 0:
        fold = cap * rest // HD
        blocks += [(whole * cap, i * fold, fold, whole * HD, i * rest, rest) for i in range(HD // rest)]
        return whole * cap + fold, blocks
    if rest:
        blocks.append((whole * cap, 0, cap, whole * HD, 0, rest))
    return (whole + (1 if rest else 0)) * cap, blocks


def pack_rows(rows, cap, width):
    _, blocks = packing(cap, width)
    pieces = {}
    for first, row, count, column, lane, columns in blocks:
        pieces.setdefault(first, []).append(rows[row : row + count, column : column + columns])
    joined = []
    for first in sorted(pieces):
        side = jnp.concatenate(pieces[first], axis=1) if len(pieces[first]) > 1 else pieces[first][0]
        if side.shape[1] < HD:
            side = jnp.concatenate([side, jnp.zeros((side.shape[0], HD - side.shape[1]), side.dtype)], axis=1)
        joined.append(side)
    return jnp.concatenate(joined, axis=0)


def unpack_rows(packed, cap, width):
    _, blocks = packing(cap, width)
    columns = {}
    for first, row, count, column, lane, wide in blocks:
        columns.setdefault(column, []).append(packed[first : first + count, lane : lane + wide])
    return [jnp.concatenate(columns[c], axis=0) for c in sorted(columns)]


def shape(*dims, dtype=BF16):
    return jax.ShapeDtypeStruct(dims, dtype)


def call(kernel, out_shape, *args, cost=None, hbm=(), out_hbm=(), grant=32, **options):
    def spec(i, arg):
        if i in hbm:
            return HBM
        return SMEM if arg.dtype == jnp.int32 and arg.ndim == 1 else VMEM

    return pl.pallas_call(
        kernel,
        out_shape=out_shape,
        in_specs=[spec(i, arg) for i, arg in enumerate(args)],
        out_specs=jax.tree.unflatten(
            jax.tree.structure(out_shape),
            [HBM if i in out_hbm else VMEM for i in range(len(jax.tree.leaves(out_shape)))],
        ),
        compiler_params=pltpu.CompilerParams(vmem_limit_bytes=grant << 20),
        cost_estimate=cost,
        **options,
    )(*args)


def exchange(value):
    return lax.all_to_all(value, "seq", split_axis=0, concat_axis=0, tiled=True)


def shift(value, mask):
    pairs = [(i, i ^ mask) for i in range(lax.axis_size("seq"))]
    return lax.ppermute(value, "seq", pairs)


def line_gather(plan, chunk):
    return [shift(chunk, step * QUAD) if step else chunk for step in range(plan.line)]


def quad_gather(low, high):
    x_low, y_high = shift(low, 1), shift(high, 2)
    x_high, y_low = shift(high, 1), shift(low, 2)
    return [(low, high), (x_low, x_high), (y_low, y_high), (shift(x_low, 2), shift(y_high, 1))]


def shards(queries, keys, values, hidden, cached, active, w_out):
    tok_dev, features = queries.shape
    devices, halves = lax.axis_size("seq"), lax.axis_size("head")
    plan = Plan(devices, tok_dev, features)
    cap, columns = plan.cap, w_out.shape[1]
    act = active.reshape(1, tok_dev)
    me = lax.axis_index("seq").astype(jnp.int32).reshape(1)
    dma = pltpu.SemaphoreType.DMA
    partial = functools.partial

    parts = math.gcd(features // HD, 5)
    wanted = ((0, 1), (0, 2), (1, 1), (1, 2), (0, 3), (1, 3))
    blocks = plan.own_heads * len(wanted)
    sent, *near_k, x_v, y_v, far_k, far_v = call(
        partial(prepare_kernel, plan, parts, wanted),
        (
            shape(devices, plan.spans * cap + 8, HD),
            *[shape(tok_dev, plan.own_heads * HD) for _ in wanted],
        ),
        act, queries, keys, values, hbm=range(4), grant=56,
        scratch_shapes=[
            pltpu.VMEM((1, tok_dev), jnp.int32),
            pltpu.VMEM((tok_dev, features), BF16),
            pltpu.VMEM((cap, features), BF16),
            dma((parts + 1,)), dma((blocks,)),
        ],
    )
    near_k = [shift(part, i + 1) for i, part in enumerate(near_k)]
    spread = exchange(sent)
    near_v = [shift(x_v, 1), shift(y_v, 2)]
    far = [shift(far_k, 3), shift(far_v, 3)]
    near, far = [near_k[0], near_v[0]], [near_k[1], near_v[1], *far]
    chunk, info = call(
        partial(compact_kernel, plan),
        (shape(plan.rows, HD), shape(2, devices, HD, dtype=F32)), me, spread,
    )
    line = line_gather(plan, chunk)
    scored = plan.own_heads * plan.tok * tok_dev

    def attend(kernel, count, out, *args, **options):
        cost = pl.CostEstimate(
            flops=4 * count * scored * HD,
            transcendentals=count * scored,
            bytes_accessed=4 * count * tok_dev * HD * plan.own_heads,
        )
        held = pltpu.VMEM((plan.line * plan.rows, HD), BF16)
        scratch = [*options.get("scratch", ()), held]
        return call(kernel, out, me, *args, cost=cost, scratch_shapes=scratch)

    scored_shape = (plan.line, plan.rows + TILE, HD)
    part = attend(
        partial(attention_kernel, plan, 1, True), 2,
        shape(*scored_shape), *line, *near, keys, values,
    )
    sums = attend(
        partial(finish_kernel, plan), 2,
        tuple(shape(plan.rows + TILE, HD) for _ in range(plan.line)),
        part, *line, *far, scratch=[pltpu.VMEM(scored_shape, BF16)],
    )
    arrived = [shift(part, step * QUAD) if step else part for step, part in enumerate(sums)]
    chunk = call(partial(line_kernel, plan), shape(plan.rows, HD), *arrived)
    low, high = call(
        partial(stack_kernel, plan), (shape(plan.half, HD), shape(plan.half, HD)),
        me, *line_gather(plan, chunk),
        scratch_shapes=[pltpu.VMEM((plan.line, plan.rows, HD), BF16)],
    )
    w_rows = w_out.T
    cost = pl.CostEstimate(
        flops=2 * plan.own_heads * plan.tok * HD * columns,
        transcendentals=0,
        bytes_accessed=2 * plan.own_heads * HD * columns,
    )
    groups = quad_gather(low, high)
    proj = None
    for step in range(QUAD - 1):
        extra = () if proj is None else (proj,)
        proj = call(
            partial(project_kernel, plan, (step,)),
            shape(plan.tok, columns, dtype=F32), me, w_rows, *groups[step], *extra, cost=cost,
        )
    terms = call(
        partial(place_kernel, plan, QUAD - 1),
        shape(devices, packing(cap, columns)[0], HD), me, w_rows, *groups[QUAD - 1], proj, info,
    )
    arrived = exchange(terms)

    half = lax.axis_index("head").astype(jnp.int32).reshape(1)
    if halves == 2:
        term_args = [arrived, lax.ppermute(arrived, "head", [(0, 1), (1, 0)])]
    else:
        split = arrived.reshape(halves, devices // halves, *arrived.shape[1:])
        term_args = [lax.all_to_all(split, "head", split_axis=0, concat_axis=0, tiled=True)]
    return call(
        partial(update_kernel, plan, halves),
        shape(tok_dev, features), half, act, *term_args, hidden, cached, out_hbm=(0,),
        scratch_shapes=[
            pltpu.VMEM((tok_dev, features), BF16),
            dma((features // math.lcm(columns, HD),)),
        ],
    )


def solution(mesh):
    placed = (
        P("seq", "head"),
        P("seq", "head"),
        P("seq", "head"),
        P("seq", "head"),
        P("seq", "head"),
        P("seq"),
        P("head", "seq"),
    )


    return jax.shard_map(
        shards, mesh=mesh, in_specs=placed, out_specs=P("seq", "head"), check_vma=False
    )
```

```python
import functools
import math

import jax
import jax.numpy as jnp
from jax import lax
from jax.experimental import pallas as pl
from jax.experimental.pallas import tpu as pltpu
from jax.sharding import PartitionSpec as P


HD = 128
TILE = 16
QUAD = 4
LOG_LANES = 32
F32 = jnp.float32
BF16 = jnp.bfloat16
VMEM = pl.BlockSpec(memory_space=pltpu.VMEM)
SMEM = pl.BlockSpec(memory_space=pltpu.SMEM)
HBM = pl.BlockSpec(memory_space=pltpu.HBM)
LANES_BOTH = (((1,), (1,)), ((), ()))
ROWS_BOTH = (((0,), (0,)), ((), ()))


def iota(shape, dim):
    return lax.broadcasted_iota(jnp.int32, shape, dim).astype(F32)


class Plan:
    def __init__(self, devices, tok_dev, features):
        assert devices % (2 * QUAD) == 0
        self.devices = devices
        self.line = devices // QUAD
        self.heads = features // HD
        self.own_heads = -(-self.heads // QUAD)
        self.cap = tok_dev // 8
        self.total = devices * tok_dev * 11 // 256
        groups = -(-self.total // TILE)
        self.tok = groups * TILE
        self.tiles = -(-self.own_heads * groups // self.line)
        self.rows = self.tiles * TILE
        self.half = self.line // 2 * self.rows
        self.spans = max(
            min((self.tiles * (line + 1) - 1) // groups, self.own_heads - 1) - self.tiles * line // groups + 1
            for line in range(self.line)
        )
        assert self.tiles <= LOG_LANES

    def head_at(self, index, quad):
        return jnp.minimum(index * QUAD + quad, self.heads - 1)

    def first_head(self, line):
        return line * self.tiles * TILE // self.tok

    def sent_heads(self, device):
        first = self.first_head(device // QUAD)
        local = [min(first + i, self.own_heads - 1) for i in range(self.spans)]
        return [min(i * QUAD + device % QUAD, self.heads - 1) for i in local]

    def head_rows(self, refs, index):
        first, last = index * self.tok, (index + 1) * self.tok
        parts = []
        for i, ref in enumerate(refs):
            low, high = max(first - i * self.half, 0), min(last - i * self.half, self.half)
            if low < high:
                parts.append(ref[low:high, :])
        return parts[0] if len(parts) == 1 else jnp.concatenate(parts, axis=0)


def own_selection(act, cap):
    tokens = act.shape[1]
    before = (iota((tokens, tokens), 0) < iota((tokens, tokens), 1)).astype(BF16)
    many = jnp.broadcast_to(act, (TILE, tokens)).astype(BF16)
    rank = jnp.dot(many, before, preferred_element_type=F32)[0:1]
    rank = jnp.where(act > 0, rank, -1.0)
    return (iota((cap, tokens), 0) == rank).astype(BF16)


def prepare_kernel(plan, parts, wanted, act_hbm, q_hbm, k_hbm, v_hbm, *refs):
    out_ref, *fetched = refs[: 1 + len(wanted)]
    act_ref, q_ref, own_ref, q_sems, in_sems = refs[1 + len(wanted) :]
    me = lax.axis_index("seq")
    heads = plan.own_heads
    arriving = []
    for (source, step), ref in zip(wanted, fetched):
        quad = lax.rem(me, QUAD) ^ step
        for i in range(heads):
            columns = pl.ds(pl.multiple_of(plan.head_at(i, quad) * HD, HD), HD)
            taken = (k_hbm, v_hbm)[source].at[:, columns]
            target = ref.at[:, i * HD : (i + 1) * HD]
            arriving.append(pltpu.make_async_copy(taken, target, in_sems.at[len(arriving)]))
    wide = q_hbm.shape[1] // parts
    columns = [slice(i * wide, (i + 1) * wide) for i in range(parts)]
    queries = [
        pltpu.make_async_copy(q_hbm.at[:, c], q_ref.at[:, c], q_sems.at[i])
        for i, c in enumerate(columns)
    ]
    first = pltpu.make_async_copy(act_hbm, act_ref, q_sems.at[parts])
    early = 2 * heads
    for copy in [first, *arriving[:early], *queries, *arriving[early:]]:
        copy.start()

    first.wait()
    act = act_ref[...].astype(F32)
    chosen = own_selection(act, plan.cap)
    count = jnp.broadcast_to(jnp.sum(act, axis=1, keepdims=True), (8, HD)).astype(BF16)
    for copy, c in zip(queries, columns):
        copy.wait()
        own_ref[:, c] = jnp.dot(chosen, q_ref[:, c], preferred_element_type=F32).astype(BF16)
    for device in range(plan.devices):
        for i, head in enumerate(plan.sent_heads(device)):
            out_ref[device, i * plan.cap : (i + 1) * plan.cap, :] = own_ref[:, head * HD : (head + 1) * HD]
        out_ref[device, plan.spans * plan.cap :, :] = count
    for copy in arriving:
        copy.wait()


def compact_kernel(plan, where_ref, in_ref, out_ref, info_ref):
    devices, cap = plan.devices, plan.cap
    count = jnp.max(in_ref[:, plan.spans * cap :, :].astype(F32), axis=1)
    earlier = (iota((devices, devices), 1) < iota((devices, devices), 0)).astype(BF16)
    offset = jnp.dot(earlier, count.astype(BF16), preferred_element_type=F32)
    info_ref[0] = count
    info_ref[1] = offset
    slots = devices * cap
    place = iota((devices, slots), 1) - iota((devices, slots), 0) * cap
    held = (place >= 0) & (place < jnp.minimum(count[:, 0:1], float(cap)))
    ranks = jnp.sum(jnp.where(held, offset[:, 0:1] + place + 1.0, 0.0), axis=0, keepdims=True) - 1.0
    ranks = jnp.where(ranks < 0, -1.0e6, ranks)
    line = where_ref[0] // QUAD
    start = line * plan.rows - plan.first_head(line) * plan.tok
    packed = jnp.zeros((plan.rows, HD), F32)
    for i in range(plan.spans):
        token = iota((plan.rows, slots), 0) + (start - i * plan.tok).astype(F32)
        pick = (token == ranks).astype(BF16)
        source = in_ref[:, i * cap : (i + 1) * cap, :].reshape(slots, HD)
        packed = packed + jnp.dot(pick, source, preferred_element_type=F32)
    out_ref[...] = packed.astype(BF16)


def pack_logs(logs):
    high = logs.astype(BF16).astype(F32)
    mid = (logs - high).astype(BF16).astype(F32)
    low = (logs - high - mid).astype(BF16).astype(F32)
    return (high + pltpu.roll(mid, LOG_LANES, 1) + pltpu.roll(low, 2 * LOG_LANES, 1)).astype(BF16)


def unpack_logs(packed):
    kept = packed.astype(F32)
    return kept + pltpu.roll(kept, HD - LOG_LANES, 1) + pltpu.roll(kept, HD - 2 * LOG_LANES, 1)


def attention_kernel(plan, fetched, own, where_ref, *refs):
    *refs, out_ref, held_ref = refs
    line_refs, refs = refs[: plan.line], refs[plan.line :]
    inv_root = 1.0 / HD**0.5
    line, quad = where_ref[0] // QUAD, where_ref[0] & (QUAD - 1)
    lane = lax.broadcasted_iota(jnp.int32, (TILE, HD), 1)
    laid = [jnp.zeros((TILE, HD), F32) for _ in range(plan.line)]
    for step, ref in enumerate(line_refs):
        held_ref[pl.ds(pl.multiple_of((line ^ step) * plan.rows, TILE), plan.rows), :] = ref[...]
    first = plan.own_heads * plan.tok
    for chunk in range(first // plan.rows, plan.line):
        low = max(first - chunk * plan.rows, 0)
        if low < plan.rows:
            out_ref[chunk, low : plan.rows, :] = jnp.zeros((plan.rows - low, HD), BF16)
    for i in range(plan.own_heads):
        query = held_ref[i * plan.tok : (i + 1) * plan.tok, :]
        pairs = []
        for j in range(fetched):
            columns = slice(i * HD, (i + 1) * HD)
            pairs.append((refs[2 * j][:, columns], refs[2 * j + 1][:, columns]))
        if own:
            k_ref, v_ref = refs[2 * fetched :]
            columns = pl.ds(pl.multiple_of(plan.head_at(i, quad) * HD, HD), HD)
            pairs.append((k_ref[:, columns], v_ref[:, columns]))
        scores = [
            lax.dot_general(query, key, LANES_BOTH, preferred_element_type=F32) * inv_root
            for key, _ in pairs
        ]
        peak = functools.reduce(jnp.maximum, [jnp.max(s, axis=1, keepdims=True) for s in scores])
        expos = [jnp.exp(s - peak) for s in scores]
        total = functools.reduce(jnp.add, [jnp.sum(e, axis=1, keepdims=True) for e in expos])
        block = functools.reduce(
            jnp.add,
            [
                jnp.dot(e.astype(BF16), value, preferred_element_type=F32)
                for e, (_, value) in zip(expos, pairs)
            ],
        )
        block = (block / total).astype(BF16)
        logs = peak + jnp.log(total)
        for tile in range(plan.tok // TILE):
            chunk, place = divmod(i * (plan.tok // TILE) + tile, plan.tiles)
            mine = slice(tile * TILE, (tile + 1) * TILE)
            out_ref[chunk, place * TILE : (place + 1) * TILE, :] = block[mine]
            laid[chunk] = jnp.where(lane == place, logs[mine], laid[chunk])
    for chunk in range(plan.line):
        out_ref[chunk, plan.rows :, :] = pack_logs(laid[chunk])


def merge(plan, parts, out_ref, keep_logs):
    rows = plan.rows
    logs = [unpack_logs(part[rows:, :]) for part in parts]
    top = functools.reduce(jnp.maximum, logs)
    weights = [jnp.exp(log - top) for log in logs]
    total = functools.reduce(jnp.add, weights)
    scale = 1.0 / total
    weights = [weight * scale for weight in weights]
    for tile in range(plan.tiles):
        mine = slice(tile * TILE, (tile + 1) * TILE)
        mixed = functools.reduce(
            jnp.add,
            [w[:, tile : tile + 1] * part[mine, :].astype(F32) for w, part in zip(weights, parts)],
        )
        out_ref[mine, :] = mixed.astype(BF16)
    if keep_logs:
        lane = lax.broadcasted_iota(jnp.int32, (TILE, HD), 1)
        out_ref[rows:, :] = pack_logs(jnp.where(lane < LOG_LANES, top + jnp.log(total), 0.0))


def split_kernel(plan, where_ref, *refs):
    parts, outs = refs[: -plan.line], refs[-plan.line :]
    line = where_ref[0] // QUAD
    for step, out_ref in enumerate(outs):
        merge(plan, [part.at[line ^ step] for part in parts], out_ref, True)


def finish_kernel(plan, where_ref, near_ref, *refs):
    *refs, part_ref, held_ref = refs
    attention_kernel(plan, 2, False, where_ref, *refs[: -plan.line], part_ref, held_ref)
    split_kernel(plan, where_ref, near_ref, part_ref, *refs[-plan.line :])


def line_kernel(plan, *refs):
    merge(plan, refs[:-1], refs[-1], False)


def stack_kernel(plan, where_ref, *refs):
    *parts, low_ref, high_ref, held_ref = refs
    line = where_ref[0] // QUAD
    for step, part in enumerate(parts):
        held_ref[line ^ step] = part[...]
    for i in range(plan.line // 2):
        low_ref[i * plan.rows : (i + 1) * plan.rows, :] = held_ref[i]
        high_ref[i * plan.rows : (i + 1) * plan.rows, :] = held_ref[plan.line // 2 + i]


def project_group(plan, quad, refs, w_ref):
    sides, weights = [], []
    for i in range(plan.own_heads):
        block = plan.head_rows(refs, i)
        if plan.own_heads * QUAD != plan.heads:
            block = jnp.where(i * QUAD + quad < plan.heads, block, jnp.zeros_like(block))
        sides.append(block)
        columns = pl.ds(pl.multiple_of(plan.head_at(i, quad) * HD, HD), HD)
        weights.append(w_ref[:, columns])
    return lax.dot_general(
        jnp.concatenate(sides, axis=1),
        jnp.concatenate(weights, axis=1),
        LANES_BOTH,
        preferred_element_type=F32,
    )


def project_kernel(plan, steps, where_ref, w_ref, *refs):
    *refs, out_ref = refs
    total = None
    if len(refs) % 2:
        *refs, sum_ref = refs
        total = sum_ref[...]
    for i, step in enumerate(steps):
        quad = (where_ref[0] & (QUAD - 1)) ^ step
        term = project_group(plan, quad, refs[2 * i : 2 * i + 2], w_ref)
        total = term if total is None else total + term
    out_ref[...] = total


def place_kernel(plan, step, where_ref, w_ref, low_ref, high_ref, sum_ref, info_ref, out_ref):
    devices, cap, tok = plan.devices, plan.cap, plan.tok
    quad = (where_ref[0] & (QUAD - 1)) ^ step
    proj = sum_ref[...] + project_group(plan, quad, (low_ref, high_ref), w_ref)
    picks = []
    for device in range(devices):
        place = iota((cap, tok), 0)
        count = info_ref[0, device : device + 1, 0:1]
        offset = info_ref[1, device : device + 1, 0:1]
        picks.append(
            ((iota((cap, tok), 1) - offset == place) & (place < count)).astype(F32).astype(BF16)
        )
    pick = jnp.concatenate(picks, axis=0)
    laid = jnp.dot(pick, proj.astype(BF16), preferred_element_type=F32)
    for device in range(devices):
        rows = laid[device * cap : (device + 1) * cap]
        out_ref[device] = pack_rows(rows, cap, w_ref.shape[0]).astype(BF16)


def update_kernel(plan, halves, half_ref, act_ref, *refs):
    *term_refs, hidden_ref, cached_ref, out_hbm, held_ref, sems = refs
    cap, width = plan.cap, hidden_ref.shape[1] * halves // plan.devices
    wide = math.lcm(width, HD)
    blocks, steps = wide // width, hidden_ref.shape[1] // wide
    chosen = own_selection(act_ref[...].astype(F32), cap)
    mask = lax.dot_general(chosen, jnp.ones((cap, HD), BF16), ROWS_BOTH, preferred_element_type=F32)
    active = mask[:, 0:1] > 0
    copies = []
    for step in range(steps):
        terms = []
        for ref in term_refs:
            if ref.ndim == 3:
                first = half_ref[0] * (plan.devices // halves) + step * blocks
                sides = [[ref[first + j] for j in range(blocks)]]
            else:
                sides = [[ref[i, step * blocks + j] for j in range(blocks)] for i in range(halves)]
            for side in sides:
                wide_rows = [c for b in side for c in unpack_rows(b.astype(F32), cap, width)]
                terms.append(jnp.concatenate(wide_rows, axis=1).astype(BF16))
        summed = lax.dot_general(
            jnp.concatenate([chosen] * len(terms), axis=0),
            jnp.concatenate(terms, axis=0),
            ROWS_BOTH,
            preferred_element_type=F32,
        )
        columns = slice(step * wide, (step + 1) * wide)
        updated = (hidden_ref[:, columns].astype(F32) + summed).astype(BF16)
        held_ref[:, columns] = jnp.where(active, updated, cached_ref[:, columns])
        copy = pltpu.make_async_copy(held_ref.at[:, columns], out_hbm.at[:, columns], sems.at[step])
        copy.start()
        copies.append(copy)
    for copy in copies:
        copy.wait()


def packing(cap, width):
    whole, rest = divmod(width, HD)
    blocks = [(i * cap, 0, cap, i * HD, 0, HD) for i in range(whole)]
    if rest and HD % rest == 0 and cap % (HD // rest * TILE) == 0:
        fold = cap * rest // HD
        blocks += [(whole * cap, i * fold, fold, whole * HD, i * rest, rest) for i in range(HD // rest)]
        return whole * cap + fold, blocks
    if rest:
        blocks.append((whole * cap, 0, cap, whole * HD, 0, rest))
    return (whole + (1 if rest else 0)) * cap, blocks


def pack_rows(rows, cap, width):
    _, blocks = packing(cap, width)
    pieces = {}
    for first, row, count, column, lane, columns in blocks:
        pieces.setdefault(first, []).append(rows[row : row + count, column : column + columns])
    joined = []
    for first in sorted(pieces):
        side = jnp.concatenate(pieces[first], axis=1) if len(pieces[first]) > 1 else pieces[first][0]
        if side.shape[1] < HD:
            side = jnp.concatenate([side, jnp.zeros((side.shape[0], HD - side.shape[1]), side.dtype)], axis=1)
        joined.append(side)
    return jnp.concatenate(joined, axis=0)


def unpack_rows(packed, cap, width):
    _, blocks = packing(cap, width)
    columns = {}
    for first, row, count, column, lane, wide in blocks:
        columns.setdefault(column, []).append(packed[first : first + count, lane : lane + wide])
    return [jnp.concatenate(columns[c], axis=0) for c in sorted(columns)]


def shape(*dims, dtype=BF16):
    return jax.ShapeDtypeStruct(dims, dtype)


def call(kernel, out_shape, *args, cost=None, hbm=(), out_hbm=(), grant=32, **options):
    def spec(i, arg):
        if i in hbm:
            return HBM
        return SMEM if arg.dtype == jnp.int32 and arg.ndim == 1 else VMEM

    return pl.pallas_call(
        kernel,
        out_shape=out_shape,
        in_specs=[spec(i, arg) for i, arg in enumerate(args)],
        out_specs=jax.tree.unflatten(
            jax.tree.structure(out_shape),
            [HBM if i in out_hbm else VMEM for i in range(len(jax.tree.leaves(out_shape)))],
        ),
        compiler_params=pltpu.CompilerParams(vmem_limit_bytes=grant << 20),
        cost_estimate=cost,
        **options,
    )(*args)


def exchange(value):
    return lax.all_to_all(value, "seq", split_axis=0, concat_axis=0, tiled=True)


def shift(value, mask):
    pairs = [(i, i ^ mask) for i in range(lax.axis_size("seq"))]
    return lax.ppermute(value, "seq", pairs)


def line_shift(parts):
    out = [parts[0]]
    for step in range(1, len(parts)):
        out.append(shift(parts[step], step * QUAD))
    return out


def line_gather(plan, chunk):
    return line_shift([chunk] * plan.line)


def quad_gather(low, high):
    x_low, y_high = shift(low, 1), shift(high, 2)
    x_high, y_low = shift(high, 1), shift(low, 2)
    return [(low, high), (x_low, x_high), (y_low, y_high), (shift(x_low, 2), shift(y_high, 1))]


def shards(queries, keys, values, hidden, cached, active, w_out):
    tok_dev, features = queries.shape
    devices, halves = lax.axis_size("seq"), lax.axis_size("head")
    plan = Plan(devices, tok_dev, features)
    cap, columns = plan.cap, w_out.shape[1]
    act = active.reshape(1, tok_dev)
    me = lax.axis_index("seq").astype(jnp.int32).reshape(1)
    dma = pltpu.SemaphoreType.DMA
    partial = functools.partial

    parts = math.gcd(features // HD, 5)
    wanted = ((0, 1), (0, 2), (1, 1), (1, 2), (0, 3), (1, 3))
    blocks = plan.own_heads * len(wanted)
    sent, *near_k, x_v, y_v, far_k, far_v = call(
        partial(prepare_kernel, plan, parts, wanted),
        (
            shape(devices, plan.spans * cap + 8, HD),
            *[shape(tok_dev, plan.own_heads * HD) for _ in wanted],
        ),
        act, queries, keys, values, hbm=range(4), grant=56,
        scratch_shapes=[
            pltpu.VMEM((1, tok_dev), jnp.int32),
            pltpu.VMEM((tok_dev, features), BF16),
            pltpu.VMEM((cap, features), BF16),
            dma((parts + 1,)), dma((blocks,)),
        ],
    )
    near_k = [shift(part, i + 1) for i, part in enumerate(near_k)]
    spread = exchange(sent)
    near_v = [shift(x_v, 1), shift(y_v, 2)]
    far = [shift(far_k, 3), shift(far_v, 3)]
    near, far = [near_k[0], near_v[0]], [near_k[1], near_v[1], *far]
    chunk, info = call(
        partial(compact_kernel, plan),
        (shape(plan.rows, HD), shape(2, devices, HD, dtype=F32)), me, spread,
    )
    line = line_gather(plan, chunk)
    scored = plan.own_heads * plan.tok * tok_dev

    def attend(kernel, count, out, *args, **options):
        cost = pl.CostEstimate(
            flops=4 * count * scored * HD,
            transcendentals=count * scored,
            bytes_accessed=4 * count * tok_dev * HD * plan.own_heads,
        )
        held = pltpu.VMEM((plan.line * plan.rows, HD), BF16)
        scratch = [*options.get("scratch", ()), held]
        return call(kernel, out, me, *args, cost=cost, scratch_shapes=scratch)

    scored_shape = (plan.line, plan.rows + TILE, HD)
    part = attend(
        partial(attention_kernel, plan, 1, True), 2,
        shape(*scored_shape), *line, *near, keys, values,
    )
    sums = attend(
        partial(finish_kernel, plan), 2,
        tuple(shape(plan.rows + TILE, HD) for _ in range(plan.line)),
        part, *line, *far, scratch=[pltpu.VMEM(scored_shape, BF16)],
    )
    arrived = line_shift(sums)
    chunk = call(partial(line_kernel, plan), shape(plan.rows, HD), *arrived)
    low, high = call(
        partial(stack_kernel, plan), (shape(plan.half, HD), shape(plan.half, HD)),
        me, *line_gather(plan, chunk),
        scratch_shapes=[pltpu.VMEM((plan.line, plan.rows, HD), BF16)],
    )
    w_rows = w_out.T
    cost = pl.CostEstimate(
        flops=2 * plan.own_heads * plan.tok * HD * columns,
        transcendentals=0,
        bytes_accessed=2 * plan.own_heads * HD * columns,
    )
    groups = quad_gather(low, high)
    proj = None
    for step in range(QUAD - 1):
        extra = () if proj is None else (proj,)
        proj = call(
            partial(project_kernel, plan, (step,)),
            shape(plan.tok, columns, dtype=F32), me, w_rows, *groups[step], *extra, cost=cost,
        )
    terms = call(
        partial(place_kernel, plan, QUAD - 1),
        shape(devices, packing(cap, columns)[0], HD), me, w_rows, *groups[QUAD - 1], proj, info,
    )
    arrived = exchange(terms)

    half = lax.axis_index("head").astype(jnp.int32).reshape(1)
    if halves == 2:
        term_args = [arrived, lax.ppermute(arrived, "head", [(0, 1), (1, 0)])]
    else:
        split = arrived.reshape(halves, devices // halves, *arrived.shape[1:])
        term_args = [lax.all_to_all(split, "head", split_axis=0, concat_axis=0, tiled=True)]
    return call(
        partial(update_kernel, plan, halves),
        shape(tok_dev, features), half, act, *term_args, hidden, cached, out_hbm=(0,),
        scratch_shapes=[
            pltpu.VMEM((tok_dev, features), BF16),
            dma((features // math.lcm(columns, HD),)),
        ],
    )


def solution(mesh):
    placed = (
        P("seq", "head"),
        P("seq", "head"),
        P("seq", "head"),
        P("seq", "head"),
        P("seq", "head"),
        P("seq"),
        P("head", "seq"),
    )


    return jax.shard_map(
        shards, mesh=mesh, in_specs=placed, out_specs=P("seq", "head"), check_vma=False
    )
```

```python
import functools
import math

import jax
import jax.numpy as jnp
from jax import lax
from jax.experimental import pallas as pl
from jax.experimental.pallas import tpu as pltpu
from jax.sharding import PartitionSpec as P


HD = 128
TILE = 16
QUAD = 4
LOG_LANES = 32
F32 = jnp.float32
BF16 = jnp.bfloat16
VMEM = pl.BlockSpec(memory_space=pltpu.VMEM)
SMEM = pl.BlockSpec(memory_space=pltpu.SMEM)
HBM = pl.BlockSpec(memory_space=pltpu.HBM)
LANES_BOTH = (((1,), (1,)), ((), ()))
ROWS_BOTH = (((0,), (0,)), ((), ()))


def iota(shape, dim):
    return lax.broadcasted_iota(jnp.int32, shape, dim).astype(F32)


class Plan:
    def __init__(self, devices, tok_dev, features):
        assert devices % (2 * QUAD) == 0
        self.devices = devices
        self.line = devices // QUAD
        self.heads = features // HD
        self.own_heads = -(-self.heads // QUAD)
        self.cap = tok_dev // 8
        self.total = devices * tok_dev * 11 // 256
        groups = -(-self.total // TILE)
        self.tok = groups * TILE
        self.tiles = -(-self.own_heads * groups // self.line)
        self.rows = self.tiles * TILE
        self.half = self.line // 2 * self.rows
        self.spans = max(
            min((self.tiles * (line + 1) - 1) // groups, self.own_heads - 1) - self.tiles * line // groups + 1
            for line in range(self.line)
        )
        assert self.tiles <= LOG_LANES

    def head_at(self, index, quad):
        return jnp.minimum(index * QUAD + quad, self.heads - 1)

    def first_head(self, line):
        return line * self.tiles * TILE // self.tok

    def sent_heads(self, device):
        first = self.first_head(device // QUAD)
        local = [min(first + i, self.own_heads - 1) for i in range(self.spans)]
        return [min(i * QUAD + device % QUAD, self.heads - 1) for i in local]

    def head_rows(self, refs, index):
        first, last = index * self.tok, (index + 1) * self.tok
        parts = []
        for i, ref in enumerate(refs):
            low, high = max(first - i * self.half, 0), min(last - i * self.half, self.half)
            if low < high:
                parts.append(ref[low:high, :])
        return parts[0] if len(parts) == 1 else jnp.concatenate(parts, axis=0)


def own_selection(act, cap):
    tokens = act.shape[1]
    before = (iota((tokens, tokens), 0) < iota((tokens, tokens), 1)).astype(BF16)
    many = jnp.broadcast_to(act, (TILE, tokens)).astype(BF16)
    rank = jnp.dot(many, before, preferred_element_type=F32)[0:1]
    rank = jnp.where(act > 0, rank, -1.0)
    return (iota((cap, tokens), 0) == rank).astype(BF16)


def prepare_kernel(plan, parts, wanted, act_hbm, q_hbm, k_hbm, v_hbm, *refs):
    out_ref, *fetched = refs[: 1 + len(wanted)]
    act_ref, q_ref, own_ref, q_sems, in_sems = refs[1 + len(wanted) :]
    me = lax.axis_index("seq")
    heads = plan.own_heads
    arriving = []
    for (source, step), ref in zip(wanted, fetched):
        quad = lax.rem(me, QUAD) ^ step
        for i in range(heads):
            columns = pl.ds(pl.multiple_of(plan.head_at(i, quad) * HD, HD), HD)
            taken = (k_hbm, v_hbm)[source].at[:, columns]
            target = ref.at[:, i * HD : (i + 1) * HD]
            arriving.append(pltpu.make_async_copy(taken, target, in_sems.at[len(arriving)]))
    wide = q_hbm.shape[1] // parts
    columns = [slice(i * wide, (i + 1) * wide) for i in range(parts)]
    queries = [
        pltpu.make_async_copy(q_hbm.at[:, c], q_ref.at[:, c], q_sems.at[i])
        for i, c in enumerate(columns)
    ]
    first = pltpu.make_async_copy(act_hbm, act_ref, q_sems.at[parts])
    early = 2 * heads
    for copy in [first, *arriving[:early], *queries, *arriving[early:]]:
        copy.start()

    first.wait()
    act = act_ref[...].astype(F32)
    chosen = own_selection(act, plan.cap)
    count = jnp.broadcast_to(jnp.sum(act, axis=1, keepdims=True), (8, HD)).astype(BF16)
    for copy, c in zip(queries, columns):
        copy.wait()
        own_ref[:, c] = jnp.dot(chosen, q_ref[:, c], preferred_element_type=F32).astype(BF16)
    for device in range(plan.devices):
        for i, head in enumerate(plan.sent_heads(device)):
            out_ref[device, i * plan.cap : (i + 1) * plan.cap, :] = own_ref[:, head * HD : (head + 1) * HD]
        out_ref[device, plan.spans * plan.cap :, :] = count
    for copy in arriving:
        copy.wait()


def compact_kernel(plan, where_ref, in_ref, out_ref, info_ref):
    devices, cap = plan.devices, plan.cap
    count = jnp.max(in_ref[:, plan.spans * cap :, :].astype(F32), axis=1)
    earlier = (iota((devices, devices), 1) < iota((devices, devices), 0)).astype(BF16)
    offset = jnp.dot(earlier, count.astype(BF16), preferred_element_type=F32)
    info_ref[0] = count
    info_ref[1] = offset
    slots = devices * cap
    place = iota((devices, slots), 1) - iota((devices, slots), 0) * cap
    held = (place >= 0) & (place < jnp.minimum(count[:, 0:1], float(cap)))
    ranks = jnp.sum(jnp.where(held, offset[:, 0:1] + place + 1.0, 0.0), axis=0, keepdims=True) - 1.0
    ranks = jnp.where(ranks < 0, -1.0e6, ranks)
    line = where_ref[0] // QUAD
    start = line * plan.rows - plan.first_head(line) * plan.tok
    packed = jnp.zeros((plan.rows, HD), F32)
    for i in range(plan.spans):
        token = iota((plan.rows, slots), 0) + (start - i * plan.tok).astype(F32)
        pick = (token == ranks).astype(BF16)
        source = in_ref[:, i * cap : (i + 1) * cap, :].reshape(slots, HD)
        packed = packed + jnp.dot(pick, source, preferred_element_type=F32)
    out_ref[...] = packed.astype(BF16)


def pack_logs(logs):
    high = logs.astype(BF16).astype(F32)
    mid = (logs - high).astype(BF16).astype(F32)
    low = (logs - high - mid).astype(BF16).astype(F32)
    return (high + pltpu.roll(mid, LOG_LANES, 1) + pltpu.roll(low, 2 * LOG_LANES, 1)).astype(BF16)


def unpack_logs(packed):
    kept = packed.astype(F32)
    return kept + pltpu.roll(kept, HD - LOG_LANES, 1) + pltpu.roll(kept, HD - 2 * LOG_LANES, 1)


def attention_kernel(plan, fetched, own, where_ref, *refs):
    *refs, out_ref, held_ref = refs
    line_refs, refs = refs[: plan.line], refs[plan.line :]
    inv_root = 1.0 / HD**0.5
    line, quad = where_ref[0] // QUAD, where_ref[0] & (QUAD - 1)
    lane = lax.broadcasted_iota(jnp.int32, (TILE, HD), 1)
    laid = [jnp.zeros((TILE, HD), F32) for _ in range(plan.line)]
    for step, ref in enumerate(line_refs):
        held_ref[pl.ds(pl.multiple_of((line ^ step) * plan.rows, TILE), plan.rows), :] = ref[...]
    first = plan.own_heads * plan.tok
    for chunk in range(first // plan.rows, plan.line):
        low = max(first - chunk * plan.rows, 0)
        if low < plan.rows:
            out_ref[chunk, low : plan.rows, :] = jnp.zeros((plan.rows - low, HD), BF16)
    for i in range(plan.own_heads):
        query = held_ref[i * plan.tok : (i + 1) * plan.tok, :]
        pairs = []
        for j in range(fetched):
            columns = slice(i * HD, (i + 1) * HD)
            pairs.append((refs[2 * j][:, columns], refs[2 * j + 1][:, columns]))
        if own:
            k_ref, v_ref = refs[2 * fetched :]
            columns = pl.ds(pl.multiple_of(plan.head_at(i, quad) * HD, HD), HD)
            pairs.append((k_ref[:, columns], v_ref[:, columns]))
        scores = [
            lax.dot_general(query, key, LANES_BOTH, preferred_element_type=F32) * inv_root
            for key, _ in pairs
        ]
        peak = functools.reduce(jnp.maximum, [jnp.max(s, axis=1, keepdims=True) for s in scores])
        expos = [jnp.exp(s - peak) for s in scores]
        total = functools.reduce(jnp.add, [jnp.sum(e, axis=1, keepdims=True) for e in expos])
        block = functools.reduce(
            jnp.add,
            [
                jnp.dot(e.astype(BF16), value, preferred_element_type=F32)
                for e, (_, value) in zip(expos, pairs)
            ],
        )
        block = (block / total).astype(BF16)
        logs = peak + jnp.log(total)
        for tile in range(plan.tok // TILE):
            chunk, place = divmod(i * (plan.tok // TILE) + tile, plan.tiles)
            mine = slice(tile * TILE, (tile + 1) * TILE)
            out_ref[chunk, place * TILE : (place + 1) * TILE, :] = block[mine]
            laid[chunk] = jnp.where(lane == place, logs[mine], laid[chunk])
    for chunk in range(plan.line):
        out_ref[chunk, plan.rows :, :] = pack_logs(laid[chunk])


def merge(plan, parts, out_ref, keep_logs):
    rows = plan.rows
    logs = [unpack_logs(part[rows:, :]) for part in parts]
    top = functools.reduce(jnp.maximum, logs)
    weights = [jnp.exp(log - top) for log in logs]
    total = functools.reduce(jnp.add, weights)
    scale = 1.0 / total
    weights = [weight * scale for weight in weights]
    for tile in range(plan.tiles):
        mine = slice(tile * TILE, (tile + 1) * TILE)
        mixed = functools.reduce(
            jnp.add,
            [w[:, tile : tile + 1] * part[mine, :].astype(F32) for w, part in zip(weights, parts)],
        )
        out_ref[mine, :] = mixed.astype(BF16)
    if keep_logs:
        lane = lax.broadcasted_iota(jnp.int32, (TILE, HD), 1)
        out_ref[rows:, :] = pack_logs(jnp.where(lane < LOG_LANES, top + jnp.log(total), 0.0))


def split_kernel(plan, where_ref, *refs):
    parts, outs = refs[: -plan.line], refs[-plan.line :]
    line = where_ref[0] // QUAD
    for step, out_ref in enumerate(outs):
        merge(plan, [part.at[line ^ step] for part in parts], out_ref, True)


def finish_kernel(plan, where_ref, near_ref, *refs):
    *refs, part_ref, held_ref = refs
    attention_kernel(plan, 1, False, where_ref, *refs[: -plan.line], part_ref, held_ref)
    split_kernel(plan, where_ref, near_ref, part_ref, *refs[-plan.line :])


def line_kernel(plan, *refs):
    merge(plan, refs[:-1], refs[-1], False)


def stack_kernel(plan, where_ref, *refs):
    *parts, low_ref, high_ref, held_ref = refs
    line = where_ref[0] // QUAD
    for step, part in enumerate(parts):
        held_ref[line ^ step] = part[...]
    for i in range(plan.line // 2):
        low_ref[i * plan.rows : (i + 1) * plan.rows, :] = held_ref[i]
        high_ref[i * plan.rows : (i + 1) * plan.rows, :] = held_ref[plan.line // 2 + i]


def project_group(plan, quad, refs, w_ref):
    sides, weights = [], []
    for i in range(plan.own_heads):
        block = plan.head_rows(refs, i)
        if plan.own_heads * QUAD != plan.heads:
            block = jnp.where(i * QUAD + quad < plan.heads, block, jnp.zeros_like(block))
        sides.append(block)
        columns = pl.ds(pl.multiple_of(plan.head_at(i, quad) * HD, HD), HD)
        weights.append(w_ref[:, columns])
    return lax.dot_general(
        jnp.concatenate(sides, axis=1),
        jnp.concatenate(weights, axis=1),
        LANES_BOTH,
        preferred_element_type=F32,
    )


def project_kernel(plan, steps, where_ref, w_ref, *refs):
    *refs, out_ref = refs
    total = None
    if len(refs) % 2:
        *refs, sum_ref = refs
        total = sum_ref[...]
    for i, step in enumerate(steps):
        quad = (where_ref[0] & (QUAD - 1)) ^ step
        term = project_group(plan, quad, refs[2 * i : 2 * i + 2], w_ref)
        total = term if total is None else total + term
    out_ref[...] = total


def place_kernel(plan, step, where_ref, w_ref, low_ref, high_ref, sum_ref, info_ref, out_ref):
    devices, cap, tok = plan.devices, plan.cap, plan.tok
    quad = (where_ref[0] & (QUAD - 1)) ^ step
    proj = sum_ref[...] + project_group(plan, quad, (low_ref, high_ref), w_ref)
    picks = []
    for device in range(devices):
        place = iota((cap, tok), 0)
        count = info_ref[0, device : device + 1, 0:1]
        offset = info_ref[1, device : device + 1, 0:1]
        picks.append(
            ((iota((cap, tok), 1) - offset == place) & (place < count)).astype(F32).astype(BF16)
        )
    pick = jnp.concatenate(picks, axis=0)
    laid = jnp.dot(pick, proj.astype(BF16), preferred_element_type=F32)
    for device in range(devices):
        rows = laid[device * cap : (device + 1) * cap]
        out_ref[device] = pack_rows(rows, cap, w_ref.shape[0]).astype(BF16)


def update_kernel(plan, halves, half_ref, act_ref, *refs):
    *term_refs, hidden_ref, cached_ref, out_hbm, held_ref, sems = refs
    cap, width = plan.cap, hidden_ref.shape[1] * halves // plan.devices
    wide = math.lcm(width, HD)
    blocks, steps = wide // width, hidden_ref.shape[1] // wide
    chosen = own_selection(act_ref[...].astype(F32), cap)
    mask = lax.dot_general(chosen, jnp.ones((cap, HD), BF16), ROWS_BOTH, preferred_element_type=F32)
    active = mask[:, 0:1] > 0
    copies = []
    for step in range(steps):
        terms = []
        for ref in term_refs:
            if ref.ndim == 3:
                first = half_ref[0] * (plan.devices // halves) + step * blocks
                sides = [[ref[first + j] for j in range(blocks)]]
            else:
                sides = [[ref[i, step * blocks + j] for j in range(blocks)] for i in range(halves)]
            for side in sides:
                wide_rows = [c for b in side for c in unpack_rows(b.astype(F32), cap, width)]
                terms.append(jnp.concatenate(wide_rows, axis=1).astype(BF16))
        summed = lax.dot_general(
            jnp.concatenate([chosen] * len(terms), axis=0),
            jnp.concatenate(terms, axis=0),
            ROWS_BOTH,
            preferred_element_type=F32,
        )
        columns = slice(step * wide, (step + 1) * wide)
        updated = (hidden_ref[:, columns].astype(F32) + summed).astype(BF16)
        held_ref[:, columns] = jnp.where(active, updated, cached_ref[:, columns])
        copy = pltpu.make_async_copy(held_ref.at[:, columns], out_hbm.at[:, columns], sems.at[step])
        copy.start()
        copies.append(copy)
    for copy in copies:
        copy.wait()


def packing(cap, width):
    whole, rest = divmod(width, HD)
    blocks = [(i * cap, 0, cap, i * HD, 0, HD) for i in range(whole)]
    if rest and HD % rest == 0 and cap % (HD // rest * TILE) == 0:
        fold = cap * rest // HD
        blocks += [(whole * cap, i * fold, fold, whole * HD, i * rest, rest) for i in range(HD // rest)]
        return whole * cap + fold, blocks
    if rest:
        blocks.append((whole * cap, 0, cap, whole * HD, 0, rest))
    return (whole + (1 if rest else 0)) * cap, blocks


def pack_rows(rows, cap, width):
    _, blocks = packing(cap, width)
    pieces = {}
    for first, row, count, column, lane, columns in blocks:
        pieces.setdefault(first, []).append(rows[row : row + count, column : column + columns])
    joined = []
    for first in sorted(pieces):
        side = jnp.concatenate(pieces[first], axis=1) if len(pieces[first]) > 1 else pieces[first][0]
        if side.shape[1] < HD:
            side = jnp.concatenate([side, jnp.zeros((side.shape[0], HD - side.shape[1]), side.dtype)], axis=1)
        joined.append(side)
    return jnp.concatenate(joined, axis=0)


def unpack_rows(packed, cap, width):
    _, blocks = packing(cap, width)
    columns = {}
    for first, row, count, column, lane, wide in blocks:
        columns.setdefault(column, []).append(packed[first : first + count, lane : lane + wide])
    return [jnp.concatenate(columns[c], axis=0) for c in sorted(columns)]


def shape(*dims, dtype=BF16):
    return jax.ShapeDtypeStruct(dims, dtype)


def call(kernel, out_shape, *args, cost=None, hbm=(), out_hbm=(), grant=32, **options):
    def spec(i, arg):
        if i in hbm:
            return HBM
        return SMEM if arg.dtype == jnp.int32 and arg.ndim == 1 else VMEM

    return pl.pallas_call(
        kernel,
        out_shape=out_shape,
        in_specs=[spec(i, arg) for i, arg in enumerate(args)],
        out_specs=jax.tree.unflatten(
            jax.tree.structure(out_shape),
            [HBM if i in out_hbm else VMEM for i in range(len(jax.tree.leaves(out_shape)))],
        ),
        compiler_params=pltpu.CompilerParams(vmem_limit_bytes=grant << 20),
        cost_estimate=cost,
        **options,
    )(*args)


def exchange(value):
    return lax.all_to_all(value, "seq", split_axis=0, concat_axis=0, tiled=True)


def shift(value, mask):
    pairs = [(i, i ^ mask) for i in range(lax.axis_size("seq"))]
    return lax.ppermute(value, "seq", pairs)


def line_shift(parts):
    out = [parts[0]]
    for step in range(1, len(parts)):
        out.append(shift(parts[step], step * QUAD))
    return out


def line_gather(plan, chunk):
    return line_shift([chunk] * plan.line)


def quad_gather(low, high):
    x_low, y_high = shift(low, 1), shift(high, 2)
    x_high, y_low = shift(high, 1), shift(low, 2)
    return [(low, high), (x_low, x_high), (y_low, y_high), (shift(x_low, 2), shift(y_high, 1))]


def shards(queries, keys, values, hidden, cached, active, w_out):
    tok_dev, features = queries.shape
    devices, halves = lax.axis_size("seq"), lax.axis_size("head")
    plan = Plan(devices, tok_dev, features)
    cap, columns = plan.cap, w_out.shape[1]
    act = active.reshape(1, tok_dev)
    me = lax.axis_index("seq").astype(jnp.int32).reshape(1)
    dma = pltpu.SemaphoreType.DMA
    partial = functools.partial

    parts = math.gcd(features // HD, 5)
    wanted = ((0, 1), (0, 2), (1, 1), (1, 2), (0, 3), (1, 3))
    blocks = plan.own_heads * len(wanted)
    sent, *near_k, x_v, y_v, far_k, far_v = call(
        partial(prepare_kernel, plan, parts, wanted),
        (
            shape(devices, plan.spans * cap + 8, HD),
            *[shape(tok_dev, plan.own_heads * HD) for _ in wanted],
        ),
        act, queries, keys, values, hbm=range(4), grant=56,
        scratch_shapes=[
            pltpu.VMEM((1, tok_dev), jnp.int32),
            pltpu.VMEM((tok_dev, features), BF16),
            pltpu.VMEM((cap, features), BF16),
            dma((parts + 1,)), dma((blocks,)),
        ],
    )
    x_k = shift(near_k[0], 1)
    y_k = shift(near_k[1], 2)
    near_k = [x_k, y_k]
    spread = exchange(sent)
    x_v = shift(x_v, 1)
    y_v = shift(y_v, 2)
    near_v = [x_v, y_v]
    far = [shift(far_k, 3), shift(far_v, 3)]
    near = [part for pair in zip(near_k, near_v) for part in pair]
    chunk, info = call(
        partial(compact_kernel, plan),
        (shape(plan.rows, HD), shape(2, devices, HD, dtype=F32)), me, spread,
    )
    line = line_gather(plan, chunk)
    scored = plan.own_heads * plan.tok * tok_dev

    def attend(kernel, count, out, *args, **options):
        cost = pl.CostEstimate(
            flops=4 * count * scored * HD,
            transcendentals=count * scored,
            bytes_accessed=4 * count * tok_dev * HD * plan.own_heads,
        )
        held = pltpu.VMEM((plan.line * plan.rows, HD), BF16)
        scratch = [*options.get("scratch", ()), held]
        return call(kernel, out, me, *args, cost=cost, scratch_shapes=scratch)

    scored_shape = (plan.line, plan.rows + TILE, HD)
    part = attend(
        partial(attention_kernel, plan, 2, True), 3,
        shape(*scored_shape), *line, *near, keys, values,
    )
    sums = attend(
        partial(finish_kernel, plan), 1,
        tuple(shape(plan.rows + TILE, HD) for _ in range(plan.line)),
        part, *line, *far, scratch=[pltpu.VMEM(scored_shape, BF16)],
    )
    arrived = line_shift(sums)
    chunk = call(partial(line_kernel, plan), shape(plan.rows, HD), *arrived)
    low, high = call(
        partial(stack_kernel, plan), (shape(plan.half, HD), shape(plan.half, HD)),
        me, *line_gather(plan, chunk),
        scratch_shapes=[pltpu.VMEM((plan.line, plan.rows, HD), BF16)],
    )
    w_rows = w_out.T
    cost = pl.CostEstimate(
        flops=2 * plan.own_heads * plan.tok * HD * columns,
        transcendentals=0,
        bytes_accessed=2 * plan.own_heads * HD * columns,
    )
    groups = quad_gather(low, high)
    proj = None
    for step in range(QUAD - 1):
        extra = () if proj is None else (proj,)
        proj = call(
            partial(project_kernel, plan, (step,)),
            shape(plan.tok, columns, dtype=F32), me, w_rows, *groups[step], *extra, cost=cost,
        )
    terms = call(
        partial(place_kernel, plan, QUAD - 1),
        shape(devices, packing(cap, columns)[0], HD), me, w_rows, *groups[QUAD - 1], proj, info,
    )
    arrived = exchange(terms)

    half = lax.axis_index("head").astype(jnp.int32).reshape(1)
    if halves == 2:
        term_args = [arrived, lax.ppermute(arrived, "head", [(0, 1), (1, 0)])]
    else:
        split = arrived.reshape(halves, devices // halves, *arrived.shape[1:])
        term_args = [lax.all_to_all(split, "head", split_axis=0, concat_axis=0, tiled=True)]
    return call(
        partial(update_kernel, plan, halves),
        shape(tok_dev, features), half, act, *term_args, hidden, cached, out_hbm=(0,),
        scratch_shapes=[
            pltpu.VMEM((tok_dev, features), BF16),
            dma((features // math.lcm(columns, HD),)),
        ],
    )


def solution(mesh):
    placed = (
        P("seq", "head"),
        P("seq", "head"),
        P("seq", "head"),
        P("seq", "head"),
        P("seq", "head"),
        P("seq"),
        P("head", "seq"),
    )


    return jax.shard_map(
        shards, mesh=mesh, in_specs=placed, out_specs=P("seq", "head"), check_vma=False
    )
```

```python
import functools
import math

import jax
import jax.numpy as jnp
from jax import lax
from jax.experimental import pallas as pl
from jax.experimental.pallas import tpu as pltpu
from jax.sharding import PartitionSpec as P


HD = 128
TILE = 16
QUAD = 4
LOG_LANES = 32
F32 = jnp.float32
BF16 = jnp.bfloat16
VMEM = pl.BlockSpec(memory_space=pltpu.VMEM)
SMEM = pl.BlockSpec(memory_space=pltpu.SMEM)
HBM = pl.BlockSpec(memory_space=pltpu.HBM)
LANES_BOTH = (((1,), (1,)), ((), ()))
ROWS_BOTH = (((0,), (0,)), ((), ()))


def iota(shape, dim):
    return lax.broadcasted_iota(jnp.int32, shape, dim).astype(F32)


class Plan:
    def __init__(self, devices, tok_dev, features):
        assert devices % (2 * QUAD) == 0
        self.devices = devices
        self.line = devices // QUAD
        self.heads = features // HD
        self.own_heads = -(-self.heads // QUAD)
        self.cap = tok_dev // 8
        self.total = devices * tok_dev * 11 // 256
        groups = -(-self.total // TILE)
        self.tok = groups * TILE
        self.tiles = -(-self.own_heads * groups // self.line)
        self.rows = self.tiles * TILE
        self.half = self.line // 2 * self.rows
        self.spans = max(
            min((self.tiles * (line + 1) - 1) // groups, self.own_heads - 1) - self.tiles * line // groups + 1
            for line in range(self.line)
        )
        assert self.tiles <= LOG_LANES

    def head_at(self, index, quad):
        return jnp.minimum(index * QUAD + quad, self.heads - 1)

    def first_head(self, line):
        return line * self.tiles * TILE // self.tok

    def sent_heads(self, device):
        first = self.first_head(device // QUAD)
        local = [min(first + i, self.own_heads - 1) for i in range(self.spans)]
        return [min(i * QUAD + device % QUAD, self.heads - 1) for i in local]

    def head_rows(self, refs, index):
        first, last = index * self.tok, (index + 1) * self.tok
        parts = []
        for i, ref in enumerate(refs):
            low, high = max(first - i * self.half, 0), min(last - i * self.half, self.half)
            if low < high:
                parts.append(ref[low:high, :])
        return parts[0] if len(parts) == 1 else jnp.concatenate(parts, axis=0)


def own_selection(act, cap):
    tokens = act.shape[1]
    before = (iota((tokens, tokens), 0) < iota((tokens, tokens), 1)).astype(BF16)
    many = jnp.broadcast_to(act, (TILE, tokens)).astype(BF16)
    rank = jnp.dot(many, before, preferred_element_type=F32)[0:1]
    rank = jnp.where(act > 0, rank, -1.0)
    return (iota((cap, tokens), 0) == rank).astype(BF16)


def prepare_kernel(plan, parts, wanted, act_hbm, q_hbm, k_hbm, v_hbm, *refs):
    out_ref, *fetched = refs[: 1 + len(wanted)]
    act_ref, q_ref, own_ref, q_sems, in_sems = refs[1 + len(wanted) :]
    me = lax.axis_index("seq")
    heads = plan.own_heads
    arriving = []
    for (source, step), ref in zip(wanted, fetched):
        quad = lax.rem(me, QUAD) ^ step
        for i in range(heads):
            columns = pl.ds(pl.multiple_of(plan.head_at(i, quad) * HD, HD), HD)
            taken = (k_hbm, v_hbm)[source].at[:, columns]
            target = ref.at[:, i * HD : (i + 1) * HD]
            arriving.append(pltpu.make_async_copy(taken, target, in_sems.at[len(arriving)]))
    wide = q_hbm.shape[1] // parts
    columns = [slice(i * wide, (i + 1) * wide) for i in range(parts)]
    queries = [
        pltpu.make_async_copy(q_hbm.at[:, c], q_ref.at[:, c], q_sems.at[i])
        for i, c in enumerate(columns)
    ]
    first = pltpu.make_async_copy(act_hbm, act_ref, q_sems.at[parts])
    early = 2 * heads
    for copy in [first, *arriving[:early], *queries, *arriving[early:]]:
        copy.start()

    first.wait()
    act = act_ref[...].astype(F32)
    chosen = own_selection(act, plan.cap)
    count = jnp.broadcast_to(jnp.sum(act, axis=1, keepdims=True), (8, HD)).astype(BF16)
    for copy, c in zip(queries, columns):
        copy.wait()
        own_ref[:, c] = jnp.dot(chosen, q_ref[:, c], preferred_element_type=F32).astype(BF16)
    for device in range(plan.devices):
        for i, head in enumerate(plan.sent_heads(device)):
            out_ref[device, i * plan.cap : (i + 1) * plan.cap, :] = own_ref[:, head * HD : (head + 1) * HD]
        out_ref[device, plan.spans * plan.cap :, :] = count
    for copy in arriving:
        copy.wait()


def compact_kernel(plan, where_ref, act_ref, in_ref, out_ref, pick_ref, chosen_ref, active_ref):
    devices, cap = plan.devices, plan.cap
    count = jnp.max(in_ref[:, plan.spans * cap :, :].astype(F32), axis=1)
    earlier = (iota((devices, devices), 1) < iota((devices, devices), 0)).astype(BF16)
    offset = jnp.dot(earlier, count.astype(BF16), preferred_element_type=F32)
    chosen = own_selection(act_ref[...].astype(F32), cap)
    chosen_ref[...] = chosen
    active_ref[...] = lax.dot_general(
        chosen, jnp.ones((cap, HD), BF16), ROWS_BOTH, preferred_element_type=F32
    )
    for device in range(devices):
        slot = iota((cap, plan.tok), 0)
        here = iota((cap, plan.tok), 1) - offset[device : device + 1, 0:1] == slot
        pick = (here & (slot < count[device : device + 1, 0:1])).astype(F32).astype(BF16)
        pick_ref[device * cap : (device + 1) * cap, :] = pick
    slots = devices * cap
    place = iota((devices, slots), 1) - iota((devices, slots), 0) * cap
    held = (place >= 0) & (place < jnp.minimum(count[:, 0:1], float(cap)))
    ranks = jnp.sum(jnp.where(held, offset[:, 0:1] + place + 1.0, 0.0), axis=0, keepdims=True) - 1.0
    ranks = jnp.where(ranks < 0, -1.0e6, ranks)
    line = where_ref[0] // QUAD
    start = line * plan.rows - plan.first_head(line) * plan.tok
    packed = jnp.zeros((plan.rows, HD), F32)
    for i in range(plan.spans):
        token = iota((plan.rows, slots), 0) + (start - i * plan.tok).astype(F32)
        pick = (token == ranks).astype(BF16)
        source = in_ref[:, i * cap : (i + 1) * cap, :].reshape(slots, HD)
        packed = packed + jnp.dot(pick, source, preferred_element_type=F32)
    out_ref[...] = packed.astype(BF16)


def pack_logs(logs):
    high = logs.astype(BF16).astype(F32)
    mid = (logs - high).astype(BF16).astype(F32)
    low = (logs - high - mid).astype(BF16).astype(F32)
    return (high + pltpu.roll(mid, LOG_LANES, 1) + pltpu.roll(low, 2 * LOG_LANES, 1)).astype(BF16)


def unpack_logs(packed):
    kept = packed.astype(F32)
    return kept + pltpu.roll(kept, HD - LOG_LANES, 1) + pltpu.roll(kept, HD - 2 * LOG_LANES, 1)


def attention_kernel(plan, fetched, own, where_ref, *refs):
    *refs, out_ref, held_ref = refs
    line_refs, refs = refs[: plan.line], refs[plan.line :]
    inv_root = 1.0 / HD**0.5
    line, quad = where_ref[0] // QUAD, where_ref[0] & (QUAD - 1)
    lane = lax.broadcasted_iota(jnp.int32, (TILE, HD), 1)
    laid = [jnp.zeros((TILE, HD), F32) for _ in range(plan.line)]
    for step, ref in enumerate(line_refs):
        held_ref[pl.ds(pl.multiple_of((line ^ step) * plan.rows, TILE), plan.rows), :] = ref[...]
    first = plan.own_heads * plan.tok
    for chunk in range(first // plan.rows, plan.line):
        low = max(first - chunk * plan.rows, 0)
        if low < plan.rows:
            out_ref[chunk, low : plan.rows, :] = jnp.zeros((plan.rows - low, HD), BF16)
    for i in range(plan.own_heads):
        query = held_ref[i * plan.tok : (i + 1) * plan.tok, :]
        pairs = []
        for j in range(fetched):
            columns = slice(i * HD, (i + 1) * HD)
            pairs.append((refs[2 * j][:, columns], refs[2 * j + 1][:, columns]))
        if own:
            k_ref, v_ref = refs[2 * fetched :]
            columns = pl.ds(pl.multiple_of(plan.head_at(i, quad) * HD, HD), HD)
            pairs.append((k_ref[:, columns], v_ref[:, columns]))
        scores = [
            lax.dot_general(query, key, LANES_BOTH, preferred_element_type=F32) * inv_root
            for key, _ in pairs
        ]
        peak = functools.reduce(jnp.maximum, [jnp.max(s, axis=1, keepdims=True) for s in scores])
        expos = [jnp.exp(s - peak) for s in scores]
        total = functools.reduce(jnp.add, [jnp.sum(e, axis=1, keepdims=True) for e in expos])
        block = functools.reduce(
            jnp.add,
            [
                jnp.dot(e.astype(BF16), value, preferred_element_type=F32)
                for e, (_, value) in zip(expos, pairs)
            ],
        )
        block = (block / total).astype(BF16)
        logs = peak + jnp.log(total)
        for tile in range(plan.tok // TILE):
            chunk, place = divmod(i * (plan.tok // TILE) + tile, plan.tiles)
            mine = slice(tile * TILE, (tile + 1) * TILE)
            out_ref[chunk, place * TILE : (place + 1) * TILE, :] = block[mine]
            laid[chunk] = jnp.where(lane == place, logs[mine], laid[chunk])
    for chunk in range(plan.line):
        out_ref[chunk, plan.rows :, :] = pack_logs(laid[chunk])


def merge(plan, parts, out_ref, keep_logs):
    rows = plan.rows
    logs = [unpack_logs(part[rows:, :]) for part in parts]
    top = functools.reduce(jnp.maximum, logs)
    weights = [jnp.exp(log - top) for log in logs]
    total = functools.reduce(jnp.add, weights)
    scale = 1.0 / total
    weights = [weight * scale for weight in weights]
    for tile in range(plan.tiles):
        mine = slice(tile * TILE, (tile + 1) * TILE)
        mixed = functools.reduce(
            jnp.add,
            [w[:, tile : tile + 1] * part[mine, :].astype(F32) for w, part in zip(weights, parts)],
        )
        out_ref[mine, :] = mixed.astype(BF16)
    if keep_logs:
        lane = lax.broadcasted_iota(jnp.int32, (TILE, HD), 1)
        out_ref[rows:, :] = pack_logs(jnp.where(lane < LOG_LANES, top + jnp.log(total), 0.0))


def split_kernel(plan, where_ref, *refs):
    parts, outs = refs[: -plan.line], refs[-plan.line :]
    line = where_ref[0] // QUAD
    for step, out_ref in enumerate(outs):
        merge(plan, [part.at[line ^ step] for part in parts], out_ref, True)


def finish_kernel(plan, where_ref, near_ref, *refs):
    *refs, part_ref, held_ref = refs
    attention_kernel(plan, 1, False, where_ref, *refs[: -plan.line], part_ref, held_ref)
    split_kernel(plan, where_ref, near_ref, part_ref, *refs[-plan.line :])


def line_kernel(plan, *refs):
    merge(plan, refs[:-1], refs[-1], False)


def stack_kernel(plan, where_ref, *refs):
    *parts, low_ref, high_ref, held_ref = refs
    line = where_ref[0] // QUAD
    for step, part in enumerate(parts):
        held_ref[line ^ step] = part[...]
    for i in range(plan.line // 2):
        low_ref[i * plan.rows : (i + 1) * plan.rows, :] = held_ref[i]
        high_ref[i * plan.rows : (i + 1) * plan.rows, :] = held_ref[plan.line // 2 + i]


def project_group(plan, quad, refs, w_ref):
    sides, weights = [], []
    for i in range(plan.own_heads):
        block = plan.head_rows(refs, i)
        if plan.own_heads * QUAD != plan.heads:
            block = jnp.where(i * QUAD + quad < plan.heads, block, jnp.zeros_like(block))
        sides.append(block)
        columns = pl.ds(pl.multiple_of(plan.head_at(i, quad) * HD, HD), HD)
        weights.append(w_ref[:, columns])
    return lax.dot_general(
        jnp.concatenate(sides, axis=1),
        jnp.concatenate(weights, axis=1),
        LANES_BOTH,
        preferred_element_type=F32,
    )


def project_kernel(plan, steps, where_ref, w_ref, *refs):
    *refs, out_ref = refs
    total = None
    if len(refs) % 2:
        *refs, sum_ref = refs
        total = sum_ref[...]
    for i, step in enumerate(steps):
        quad = (where_ref[0] & (QUAD - 1)) ^ step
        term = project_group(plan, quad, refs[2 * i : 2 * i + 2], w_ref)
        total = term if total is None else total + term
    out_ref[...] = total


def place_kernel(plan, step, where_ref, w_ref, low_ref, high_ref, sum_ref, pick_ref, out_ref):
    devices, cap = plan.devices, plan.cap
    quad = (where_ref[0] & (QUAD - 1)) ^ step
    proj = sum_ref[...] + project_group(plan, quad, (low_ref, high_ref), w_ref)
    laid = jnp.dot(pick_ref[...], proj.astype(BF16), preferred_element_type=F32)
    for device in range(devices):
        rows = laid[device * cap : (device + 1) * cap]
        out_ref[device] = pack_rows(rows, cap, w_ref.shape[0]).astype(BF16)


def update_kernel(plan, halves, half_ref, chosen_ref, active_ref, *refs):
    *term_refs, hidden_ref, cached_ref, out_hbm, held_ref, sems = refs
    cap, width = plan.cap, hidden_ref.shape[1] * halves // plan.devices
    wide = math.lcm(width, HD)
    blocks, steps = wide // width, hidden_ref.shape[1] // wide
    chosen = chosen_ref[...]
    active = active_ref[:, 0:1] > 0
    copies = []
    for step in range(steps):
        terms = []
        for ref in term_refs:
            if ref.ndim == 3:
                first = half_ref[0] * (plan.devices // halves) + step * blocks
                sides = [[ref[first + j] for j in range(blocks)]]
            else:
                sides = [[ref[i, step * blocks + j] for j in range(blocks)] for i in range(halves)]
            for side in sides:
                wide_rows = [c for b in side for c in unpack_rows(b.astype(F32), cap, width)]
                terms.append(jnp.concatenate(wide_rows, axis=1).astype(BF16))
        summed = lax.dot_general(
            jnp.concatenate([chosen] * len(terms), axis=0),
            jnp.concatenate(terms, axis=0),
            ROWS_BOTH,
            preferred_element_type=F32,
        )
        columns = slice(step * wide, (step + 1) * wide)
        updated = (hidden_ref[:, columns].astype(F32) + summed).astype(BF16)
        held_ref[:, columns] = jnp.where(active, updated, cached_ref[:, columns])
        copy = pltpu.make_async_copy(held_ref.at[:, columns], out_hbm.at[:, columns], sems.at[step])
        copy.start()
        copies.append(copy)
    for copy in copies:
        copy.wait()


def packing(cap, width):
    whole, rest = divmod(width, HD)
    blocks = [(i * cap, 0, cap, i * HD, 0, HD) for i in range(whole)]
    if rest and HD % rest == 0 and cap % (HD // rest * TILE) == 0:
        fold = cap * rest // HD
        blocks += [(whole * cap, i * fold, fold, whole * HD, i * rest, rest) for i in range(HD // rest)]
        return whole * cap + fold, blocks
    if rest:
        blocks.append((whole * cap, 0, cap, whole * HD, 0, rest))
    return (whole + (1 if rest else 0)) * cap, blocks


def pack_rows(rows, cap, width):
    _, blocks = packing(cap, width)
    pieces = {}
    for first, row, count, column, lane, columns in blocks:
        pieces.setdefault(first, []).append(rows[row : row + count, column : column + columns])
    joined = []
    for first in sorted(pieces):
        side = jnp.concatenate(pieces[first], axis=1) if len(pieces[first]) > 1 else pieces[first][0]
        if side.shape[1] < HD:
            side = jnp.concatenate([side, jnp.zeros((side.shape[0], HD - side.shape[1]), side.dtype)], axis=1)
        joined.append(side)
    return jnp.concatenate(joined, axis=0)


def unpack_rows(packed, cap, width):
    _, blocks = packing(cap, width)
    columns = {}
    for first, row, count, column, lane, wide in blocks:
        columns.setdefault(column, []).append(packed[first : first + count, lane : lane + wide])
    return [jnp.concatenate(columns[c], axis=0) for c in sorted(columns)]


def shape(*dims, dtype=BF16):
    return jax.ShapeDtypeStruct(dims, dtype)


def call(kernel, out_shape, *args, cost=None, hbm=(), out_hbm=(), grant=32, **options):
    def spec(i, arg):
        if i in hbm:
            return HBM
        return SMEM if arg.dtype == jnp.int32 and arg.ndim == 1 else VMEM

    return pl.pallas_call(
        kernel,
        out_shape=out_shape,
        in_specs=[spec(i, arg) for i, arg in enumerate(args)],
        out_specs=jax.tree.unflatten(
            jax.tree.structure(out_shape),
            [HBM if i in out_hbm else VMEM for i in range(len(jax.tree.leaves(out_shape)))],
        ),
        compiler_params=pltpu.CompilerParams(vmem_limit_bytes=grant << 20),
        cost_estimate=cost,
        **options,
    )(*args)


def exchange(value):
    return lax.all_to_all(value, "seq", split_axis=0, concat_axis=0, tiled=True)


def shift(value, mask):
    pairs = [(i, i ^ mask) for i in range(lax.axis_size("seq"))]
    return lax.ppermute(value, "seq", pairs)


def line_shift(parts):
    out = [parts[0]]
    for step in range(1, len(parts)):
        out.append(shift(parts[step], step * QUAD))
    return out


def line_gather(plan, chunk):
    return line_shift([chunk] * plan.line)


def quad_gather(low, high):
    x_low, y_high = shift(low, 1), shift(high, 2)
    x_high, y_low = shift(high, 1), shift(low, 2)
    return [(low, high), (x_low, x_high), (y_low, y_high), (shift(x_low, 2), shift(y_high, 1))]


def shards(queries, keys, values, hidden, cached, active, w_out):
    tok_dev, features = queries.shape
    devices, halves = lax.axis_size("seq"), lax.axis_size("head")
    plan = Plan(devices, tok_dev, features)
    cap, columns = plan.cap, w_out.shape[1]
    act = active.reshape(1, tok_dev)
    me = lax.axis_index("seq").astype(jnp.int32).reshape(1)
    dma = pltpu.SemaphoreType.DMA
    partial = functools.partial

    parts = math.gcd(features // HD, 5)
    wanted = ((0, 1), (0, 2), (1, 1), (1, 2), (0, 3), (1, 3))
    blocks = plan.own_heads * len(wanted)
    sent, *near_k, x_v, y_v, far_k, far_v = call(
        partial(prepare_kernel, plan, parts, wanted),
        (
            shape(devices, plan.spans * cap + 8, HD),
            *[shape(tok_dev, plan.own_heads * HD) for _ in wanted],
        ),
        act, queries, keys, values, hbm=range(4), grant=56,
        scratch_shapes=[
            pltpu.VMEM((1, tok_dev), jnp.int32),
            pltpu.VMEM((tok_dev, features), BF16),
            pltpu.VMEM((cap, features), BF16),
            dma((parts + 1,)), dma((blocks,)),
        ],
    )
    x_k = shift(near_k[0], 1)
    y_k = shift(near_k[1], 2)
    near_k = [x_k, y_k]
    spread = exchange(sent)
    x_v = shift(x_v, 1)
    y_v = shift(y_v, 2)
    near_v = [x_v, y_v]
    far = [shift(far_k, 3), shift(far_v, 3)]
    near = [part for pair in zip(near_k, near_v) for part in pair]
    chunk, pick, chosen, is_active = call(
        partial(compact_kernel, plan),
        (
            shape(plan.rows, HD), shape(devices * cap, plan.tok), shape(cap, tok_dev),
            shape(tok_dev, HD, dtype=F32),
        ),
        me, act, spread,
    )
    line = line_gather(plan, chunk)
    scored = plan.own_heads * plan.tok * tok_dev

    def attend(kernel, count, out, *args, **options):
        cost = pl.CostEstimate(
            flops=4 * count * scored * HD,
            transcendentals=count * scored,
            bytes_accessed=4 * count * tok_dev * HD * plan.own_heads,
        )
        held = pltpu.VMEM((plan.line * plan.rows, HD), BF16)
        scratch = [*options.get("scratch", ()), held]
        return call(kernel, out, me, *args, cost=cost, scratch_shapes=scratch)

    scored_shape = (plan.line, plan.rows + TILE, HD)
    part = attend(
        partial(attention_kernel, plan, 2, True), 3,
        shape(*scored_shape), *line, *near, keys, values,
    )
    sums = attend(
        partial(finish_kernel, plan), 1,
        tuple(shape(plan.rows + TILE, HD) for _ in range(plan.line)),
        part, *line, *far, scratch=[pltpu.VMEM(scored_shape, BF16)],
    )
    arrived = line_shift(sums)
    chunk = call(partial(line_kernel, plan), shape(plan.rows, HD), *arrived)
    low, high = call(
        partial(stack_kernel, plan), (shape(plan.half, HD), shape(plan.half, HD)),
        me, *line_gather(plan, chunk),
        scratch_shapes=[pltpu.VMEM((plan.line, plan.rows, HD), BF16)],
    )
    w_rows = w_out.T
    cost = pl.CostEstimate(
        flops=2 * plan.own_heads * plan.tok * HD * columns,
        transcendentals=0,
        bytes_accessed=2 * plan.own_heads * HD * columns,
    )
    groups = quad_gather(low, high)
    proj = None
    for step in range(QUAD - 1):
        extra = () if proj is None else (proj,)
        proj = call(
            partial(project_kernel, plan, (step,)),
            shape(plan.tok, columns, dtype=F32), me, w_rows, *groups[step], *extra, cost=cost,
        )
    terms = call(
        partial(place_kernel, plan, QUAD - 1),
        shape(devices, packing(cap, columns)[0], HD), me, w_rows, *groups[QUAD - 1], proj, pick,
    )
    arrived = exchange(terms)

    half = lax.axis_index("head").astype(jnp.int32).reshape(1)
    if halves == 2:
        term_args = [arrived, lax.ppermute(arrived, "head", [(0, 1), (1, 0)])]
    else:
        split = arrived.reshape(halves, devices // halves, *arrived.shape[1:])
        term_args = [lax.all_to_all(split, "head", split_axis=0, concat_axis=0, tiled=True)]
    return call(
        partial(update_kernel, plan, halves),
        shape(tok_dev, features), half, chosen, is_active, *term_args, hidden, cached, out_hbm=(0,),
        scratch_shapes=[
            pltpu.VMEM((tok_dev, features), BF16),
            dma((features // math.lcm(columns, HD),)),
        ],
    )


def solution(mesh):
    placed = (
        P("seq", "head"),
        P("seq", "head"),
        P("seq", "head"),
        P("seq", "head"),
        P("seq", "head"),
        P("seq"),
        P("head", "seq"),
    )


    return jax.shard_map(
        shards, mesh=mesh, in_specs=placed, out_specs=P("seq", "head"), check_vma=False
    )
```
